32 devices in a mesh: group: 2 (over y), ctx: 4 (over z), head: 2 (over x), req: 2 (over core).
Axes of the slice: x: 2, y: 2, z: 4, core: 2. Of those that a mesh axis runs over, the one named last changes fastest.
Arguments:
- kda_query: bfloat16 [4, 768, 4096], P(('group', 'req'), 'ctx', 'head'), parts along dimension 0, may hold values from -6 to 6
- kda_key: bfloat16 [4, 768, 4096], P(('group', 'req'), 'ctx', 'head'), parts along dimension 0, may hold values from -6 to 6
- kda_value: bfloat16 [4, 768, 4096], P(('group', 'req'), 'ctx', 'head'), parts along dimension 0, may hold values from -6 to 6
- log_decay: bfloat16 [4, 768, 4096], P(('group', 'req'), 'ctx', 'head'), parts along dimension 0, may hold values from -1 to 0
- write_strength: float32 [4, 32, 768], P(('group', 'req'), 'head', 'ctx'), parts along dimension 0, may hold values from 0.1 to 0.95
- mla_query: bfloat16 [4, 768, 18432], P(('group', 'req'), 'ctx', 'head'), parts along dimension 0, may hold values from -18 to 18
- latents: bfloat16 [4, 768, 576], P(('group', 'req'), 'ctx'), parts along dimension 0, may hold values from -8 to 8
- value_up: bfloat16 [32, 512, 128], P('head'), may hold values from -0.25 to 0.25
- out_proj: bfloat16 [4096, 2304], P('head'), may hold values from -0.09375 to 0.09375
- doc_lengths: int32 [4, 8], P(('group', 'req')), parts along dimension 0, may hold values from 1 to 288, 768 in all within a row
Outputs:
- kda_out: bfloat16 [4, 768, 4096], P(('group', 'req'), 'ctx', 'head'), parts along dimension 0
- mixed: bfloat16 [4, 768, 2304], P(('group', 'req'), ('ctx', 'head')), parts along dimension 0
The draws below stay inside these ranges and needn't reach their ends.
There are 2 independent parts, one for each index of `group`. The reference program is written for one: setup_inputs(seed, part) draws one part's arguments, and reference() takes and returns one part's arrays. A program takes and returns all parts, laid end to end along the dimension named above; an argument that names none is the same for every part. Nothing has to cross between parts.
Inputs may be any that keep to these rules, and one draw needn't show every extreme that they name: `doc_lengths`: each row's lengths sum to 768, and each row's longest prompt has exactly 288 positions.
All inputs are finite; a program needn't handle non-finite values.
Results may differ from the reference program's by a relative error of at most 0.009.
Values may be sent and summed in bfloat16 or wider, within the bound.
A program may use at most 128 MiB of HBM per device.

```python
import math
import jax
import jax.numpy as jnp
import numpy as np
from jax import lax

HEAD_COUNT = 32
STATE = 128
LATENT = 512
ROPE = 64
NOPE = 128
VHEAD = 128
MODEL = 2304
TOK_DEV = 192
DOCS = 8
PACKED_ROWS = 2
ROW_LENGTH = 768


def draw_log_decay(key, part):
    base = jax.random.fold_in(key, 3)
    piece_keys = jax.random.split(base, 8)
    fast_share = 0.5
    is_fast = jax.random.bernoulli(piece_keys[0], fast_share, (HEAD_COUNT,))
    fast_rate = jnp.exp(jax.random.uniform(piece_keys[1], (HEAD_COUNT,), jnp.float32, math.log(1.0 / 50.0), math.log(1.0 / 30.0)))
    slow_rate = jnp.exp(jax.random.uniform(piece_keys[2], (HEAD_COUNT,), jnp.float32, math.log(0.02), math.log(0.2))) / ROW_LENGTH
    head_rate = jnp.where(is_fast, fast_rate, slow_rate)
    channel_factor = jnp.exp(jax.random.uniform(piece_keys[3], (HEAD_COUNT, STATE), jnp.float32, math.log(0.6), math.log(1.6)))
    blocks_total = ROW_LENGTH // TOK_DEV
    block_multiplier = jnp.exp(jax.random.uniform(piece_keys[4], (PACKED_ROWS, blocks_total, 1, 1), jnp.float32, math.log(0.6), math.log(1.6)))
    block_multiplier = jnp.repeat(block_multiplier, TOK_DEV, axis=1)
    small_noise = jax.random.uniform(piece_keys[5], (PACKED_ROWS, ROW_LENGTH, HEAD_COUNT, STATE), jnp.float32, 0.5, 1.5)
    surge_positions = jax.random.randint(piece_keys[6], (PACKED_ROWS, 3), 0, ROW_LENGTH)
    position_list = jnp.arange(ROW_LENGTH, dtype=jnp.int32)
    surging_flag = jnp.any(surge_positions[:, None, :] == position_list[None, :, None], axis=2).astype(jnp.float32)
    surge_depth = jax.random.uniform(piece_keys[7], (PACKED_ROWS, ROW_LENGTH, HEAD_COUNT, 1), jnp.float32, 0.223, 0.693)
    decay_rates = (head_rate[:, None] * channel_factor)[None, None]
    layer_result = -(decay_rates * block_multiplier * small_noise) - surging_flag[:, :, None, None] * surge_depth
    return layer_result.reshape(PACKED_ROWS, ROW_LENGTH, HEAD_COUNT * STATE).astype(jnp.bfloat16)


def mla_pair(key):
    width = LATENT + ROPE
    key_latent = jax.random.fold_in(key, 21)
    key_query = jax.random.fold_in(key, 22)
    latent_rows = jax.random.truncated_normal(key_latent, -4.0, 4.0, (PACKED_ROWS, ROW_LENGTH, width), jnp.float32)
    query_rows = jax.random.truncated_normal(key_query, -4.0, 4.0, (PACKED_ROWS, ROW_LENGTH, HEAD_COUNT, width), jnp.float32)
    return (query_rows.reshape(PACKED_ROWS, ROW_LENGTH, HEAD_COUNT * width), latent_rows)


def draw_mla_query(key, part):
    return mla_pair(key)[0].astype(jnp.bfloat16)


def draw_latents(key, part):
    return mla_pair(key)[1].astype(jnp.bfloat16)


def shard_levels(own_key, dims, cuts, smallest, high):
    factor_of, own = 1.0, jax.random.fold_in(own_key, 6)
    for dim, shards_of in cuts:
        heights = jnp.exp(jax.random.uniform(jax.random.fold_in(own, dim), (shards_of,), jnp.float32, smallest / len(cuts), high / len(cuts)))
        factor_of = factor_of * jnp.repeat(heights, dims[dim] // shards_of).reshape([-1 if axis == dim else 1 for axis in range(len(dims))])
    return factor_of


def profile(amount, total, most, slope):
    loads = [(1 << 20) // math.isqrt(standing ** slope) + 1 for standing in range(2, amount + 1)]
    rest, counts = total - most - (amount - 1), [1] * (amount - 1)
    while rest > 0:
        free = [i for i in range(amount - 1) if counts[i] < most]
        whole, budget = sum([loads[i] for i in free]), rest
        for i in free:
            more = min(most - counts[i], max(1, budget * loads[i] // whole), rest)
            counts[i] = counts[i] + more
            rest = rest - more
    return np.array([most] + counts)


def ragged(stream_key, number_of, total, bound, slope):
    if number_of == 2:
        one = jax.random.randint(stream_key, (), max(1, total - bound), min(bound, total - 1) + 1)
        return jnp.stack([one, total - one])
    sizes = jnp.asarray(profile(number_of, total, bound, slope), jnp.int32)
    twos = (number_of - 1) // 2
    donor, taker = sizes[1:1 + 2 * twos:2], sizes[2:2 + 2 * twos:2]
    room = jnp.minimum(donor - 1, bound - taker)
    moved = jax.random.randint(jax.random.fold_in(stream_key, 1), (twos,), 0, 1 << 20) % (room + 1)
    sizes = sizes.at[1:1 + 2 * twos:2].set(donor - moved).at[2:2 + 2 * twos:2].set(taker + moved)
    return sizes[jax.random.permutation(jax.random.fold_in(stream_key, 2), number_of)]


def noise(own_key, extent, scale, bound, pieces=(), kind=jnp.bfloat16):
    values = jax.random.normal(own_key, extent, jnp.float32) * scale
    if len(pieces) > 0:
        values = shard_levels(own_key, extent, pieces, -0.22, 0.18) * values
    return jnp.clip(values, min=-bound, max=bound).astype(kind)


def setup_inputs(seed: int = 0, part: int = 0) -> dict:
    key_of = jax.random.split(jax.random.key(seed), 11)
    own_keys = jax.random.split(jax.random.fold_in(key_of[10], part), 11)
    return {
        "kda_query": noise(own_keys[0], (PACKED_ROWS, ROW_LENGTH, HEAD_COUNT * STATE), 1.0, 6.0, ((0, 2), (1, 4), (2, 2))),
        "kda_key": noise(own_keys[1], (PACKED_ROWS, ROW_LENGTH, HEAD_COUNT * STATE), 1.0, 6.0, ((0, 2), (1, 4), (2, 2))),
        "kda_value": noise(own_keys[2], (PACKED_ROWS, ROW_LENGTH, HEAD_COUNT * STATE), 1.0, 6.0, ((0, 2), (1, 4), (2, 2))),
        "log_decay": draw_log_decay(jax.random.fold_in(jax.random.fold_in(key_of[10], part), 71), part),
        "write_strength": jnp.clip(0.1 + 0.84999999 * jax.random.uniform(own_keys[4], (PACKED_ROWS, HEAD_COUNT, ROW_LENGTH), jnp.float32) ** shard_levels(own_keys[4], (PACKED_ROWS, HEAD_COUNT, ROW_LENGTH), ((0, 2), (1, 2), (2, 4)), -0.2, 0.2), 0.1, 0.95),
        "mla_query": draw_mla_query(jax.random.fold_in(jax.random.fold_in(key_of[10], part), 71), part),
        "latents": draw_latents(jax.random.fold_in(jax.random.fold_in(key_of[10], part), 71), part),
        "value_up": noise(key_of[7], (HEAD_COUNT, LATENT, VHEAD), LATENT ** -0.5, 0.25, ((0, 2),)),
        "out_proj": noise(key_of[8], (HEAD_COUNT * VHEAD, MODEL), (HEAD_COUNT * VHEAD) ** -0.5, 0.09375, ((0, 2),)),
        "doc_lengths": jax.vmap(lambda own: ragged(own, DOCS, ROW_LENGTH, 3 * ROW_LENGTH // DOCS, 2))(jax.random.split(own_keys[9], PACKED_ROWS)).reshape((PACKED_ROWS, DOCS)).astype(jnp.int32),
    }


top_value = lax.Precision.HIGHEST
masked_score = -1e+30

def unit_length(values):
    values = values.astype(jnp.float32)
    return values * lax.rsqrt(lax.optimization_barrier(jnp.sum(values * values, axis=-1, keepdims=True)) + 1e-06)

def reference(kda_query, kda_key, kda_value, log_decay, write_strength, mla_query, latents, value_up, out_proj, doc_lengths):
    positions = jnp.arange(ROW_LENGTH, dtype=jnp.int32)
    doc_ends = jnp.cumsum(doc_lengths, axis=1).astype(jnp.int32)
    doc_starts = (doc_ends - doc_lengths).astype(jnp.int32)
    doc_ids = lax.optimization_barrier(jnp.sum((doc_ends[:, None, :] <= positions[None, :, None]).astype(jnp.int32), axis=2)).astype(jnp.int32)
    opening = jnp.any(doc_starts[:, None, :] == positions[None, :, None], axis=2)
    head_shape = (PACKED_ROWS, ROW_LENGTH, HEAD_COUNT, STATE)
    query_rows = unit_length(kda_query.reshape(head_shape))
    key_rows = unit_length(kda_key.reshape(head_shape))
    value_rows = kda_value.reshape(head_shape).astype(jnp.float32)
    gate_rows = jnp.exp(log_decay.reshape(head_shape).astype(jnp.float32))
    strength = jnp.transpose(write_strength, (0, 2, 1)).astype(jnp.float32)

    def advance(state_now, inputs):
        query_t, key_t, value_t, gate_t, beta_t, open_t = inputs
        state_now = jnp.where(open_t[:, None, None, None], jnp.zeros_like(state_now), gate_t[..., None] * state_now)
        recalled = jnp.einsum('shk,shkv->shv', key_t, state_now, precision=top_value)
        state_now = state_now + beta_t[..., None, None] * key_t[..., None] * (value_t - recalled)[..., None, :]
        return (state_now, jnp.einsum('shk,shkv->shv', query_t, state_now, precision=top_value))
    stepwise = tuple((jnp.moveaxis(member, 1, 0) for member in (query_rows, key_rows, value_rows, gate_rows, strength, opening)))
    start_state = jnp.zeros((PACKED_ROWS, HEAD_COUNT, STATE, STATE), jnp.float32)
    _, outputs = lax.scan(advance, start_state, stepwise)
    kda_out = jnp.moveaxis(outputs, 0, 1).reshape(PACKED_ROWS, ROW_LENGTH, HEAD_COUNT * STATE).astype(jnp.bfloat16)
    width = LATENT + ROPE
    score_scale = 1.0 / math.sqrt(NOPE + ROPE)
    causal = positions[None, :, None] >= positions[None, None, :]
    allowed = causal & (doc_ids[:, :, None] == doc_ids[:, None, :])
    latent_rows = latents.astype(jnp.float32)
    query_heads = jnp.moveaxis(mla_query.reshape(PACKED_ROWS, ROW_LENGTH, HEAD_COUNT, width), 2, 0)

    def one_head(query_head):
        scores = jnp.einsum('sik,sjk->sij', query_head.astype(jnp.float32), latent_rows) * score_scale
        row_peak = lax.optimization_barrier(jnp.max(jnp.where(allowed, scores, masked_score), axis=2, keepdims=True))
        exponent = jnp.where(allowed, jnp.exp(scores - row_peak), jnp.zeros_like(scores))
        row_total = lax.optimization_barrier(jnp.sum(exponent, axis=2, keepdims=True))
        weights = lax.optimization_barrier(exponent.astype(jnp.bfloat16)).astype(jnp.float32)
        mixed_lat = jnp.einsum('sij,sjl->sil', weights, latent_rows[:, :, :LATENT]) / row_total
        return mixed_lat.astype(jnp.bfloat16)
    context = lax.map(one_head, query_heads)
    head_out = jnp.einsum('hsil,hlv->sihv', context.astype(jnp.float32), value_up.astype(jnp.float32)).astype(jnp.bfloat16)
    head_out = head_out.reshape(PACKED_ROWS * ROW_LENGTH, HEAD_COUNT * VHEAD)
    mixed = jnp.dot(head_out, out_proj, preferred_element_type=jnp.float32).astype(jnp.bfloat16)
    return (kda_out, mixed.reshape(PACKED_ROWS, ROW_LENGTH, MODEL))
```

```python
import math

import jax
import jax.numpy as jnp
from jax import lax
from jax.sharding import PartitionSpec as P

ROPE = 64
NOPE = 128
SPAN = 64


top_value = lax.Precision.HIGHEST
masked_score = -1e30


def from_behind(value, axis, by):
    peers = lax.axis_size(axis)
    pairs = [(i, i + by) for i in range(peers) if 0 <= i + by < peers]
    return lax.ppermute(value, axis, pairs)


def unit_length(values):
    return values * lax.rsqrt(jnp.sum(values * values, axis=-1, keepdims=True) + 1e-06)


def doc_index(position_list, doc_ends):
    return jnp.sum((doc_ends[None, :] <= position_list[:, None]).astype(jnp.int32), axis=1)


def unit_lower_inverse(lower):
    size = lower.shape[-1]
    row = jnp.arange(size, dtype=jnp.int32)[:, None]
    col = jnp.arange(size, dtype=jnp.int32)[None, :]
    inverse = jnp.broadcast_to(jnp.eye(size, dtype=jnp.float32), lower.shape)
    width = 1
    while width < size:
        corner = (row // (2 * width) == col // (2 * width)) & (row // width > col // width)
        part = jnp.where(corner[None], lower, 0.0)
        if width == 1:
            inverse = inverse - part
        else:
            half = jnp.einsum("hij,hjk->hik", inverse, part, precision=top_value)
            inverse = inverse - jnp.einsum("hij,hjk->hik", half, inverse, precision=top_value)
        width *= 2
    return inverse


def span_terms(query_rows, key_rows, value_rows, decay_rows, strength, doc_ids, prev_doc):
    span_len = key_rows.shape[1]
    state_dim = key_rows.shape[2]
    row_index = jnp.arange(span_len, dtype=jnp.int32)
    inclusive = (row_index[:, None] >= row_index[None, :]).astype(jnp.float32)
    summed = jnp.einsum("ij,hjc->hic", inclusive, decay_rows, precision=top_value)
    growth = jnp.exp(summed)
    key_hat = key_rows * growth
    key_tilde = key_rows * jnp.exp(-summed)
    query_estimate = query_rows * growth
    same_doc = doc_ids[:, None] == doc_ids[None, :]
    strict = same_doc & (row_index[:, None] > row_index[None, :])
    up_to = same_doc & (row_index[:, None] >= row_index[None, :])
    carried = (doc_ids == prev_doc).astype(jnp.float32)
    inner = jnp.einsum("hic,hjc->hij", key_hat, key_tilde, precision=top_value)
    lower_part = jnp.where(strict[None], inner * strength[:, :, None], 0.0)
    right_side = jnp.concatenate(
        [(strength * carried[None])[:, :, None] * key_hat, strength[:, :, None] * value_rows],
        axis=2,
    )
    solved = jnp.einsum(
        "hij,hjc->hic", unit_lower_inverse(lower_part), right_side, precision=top_value
    )
    weighted_key_rows = solved[:, :, :state_dim]
    update_rows = solved[:, :, state_dim:]
    attend = jnp.where(
        up_to[None], jnp.einsum("hic,hjc->hij", query_estimate, key_tilde, precision=top_value), 0.0
    )
    tail_mask = same_doc[span_len - 1].astype(jnp.float32)
    key_decay = key_rows * jnp.exp(summed[:, span_len - 1 :, :] - summed) * tail_mask[None, :, None]
    diagonal = (
        carried[span_len - 1]
        * growth[:, span_len - 1, :, None]
        * jnp.eye(state_dim, dtype=jnp.float32)[None]
    )
    transition = diagonal - jnp.einsum(
        "hjc,hjd->hcd", key_decay, weighted_key_rows, precision=top_value
    )
    offset = jnp.einsum("hjc,hjv->hcv", key_decay, update_rows, precision=top_value)
    return (query_estimate, carried, weighted_key_rows, update_rows, attend, transition, offset)


def span_output(terms, inbound_state):
    query_estimate, carried, weighted_key_rows, update_rows, attend, transition, offset = terms
    adjusted_rows = update_rows - jnp.einsum(
        "izy,iyn->izn", weighted_key_rows, inbound_state, precision=top_value
    )
    state_contribution = jnp.einsum(
        "izy,iyn->izn", query_estimate, inbound_state, precision=top_value
    )
    return carried[None, :, None] * state_contribution + jnp.einsum(
        "hij,hjv->hiv", attend, adjusted_rows, precision=top_value
    )


def apply_map(transition, offset, inbound_state):
    return jnp.einsum("hcd,hdv->hcv", transition, inbound_state, precision=top_value) + offset


def local(
    kda_query,
    kda_key,
    kda_value,
    log_decay,
    write_strength,
    mla_query,
    latents,
    value_up,
    out_proj,
    doc_lengths,
):
    tokens_dev = kda_query.shape[1]
    heads_dev = write_strength.shape[1]
    state_dim = kda_query.shape[2] // heads_dev
    ctx_count = lax.axis_size("ctx")
    ctx_place = lax.axis_index("ctx")
    first_pos = ctx_place * tokens_dev
    positions = first_pos + jnp.arange(tokens_dev, dtype=jnp.int32)
    doc_ends = jnp.cumsum(doc_lengths[0])
    doc_ids = doc_index(positions, doc_ends)

    def head_first(packed):
        return jnp.transpose(
            packed[0].astype(jnp.float32).reshape(tokens_dev, heads_dev, state_dim), (1, 0, 2)
        )

    query_rows = unit_length(head_first(kda_query))
    key_rows = unit_length(head_first(kda_key))
    value_rows = head_first(kda_value)
    decay_rows = head_first(log_decay)
    strength = write_strength[0]
    span_list = []
    eye_batch = jnp.broadcast_to(
        jnp.eye(state_dim, dtype=jnp.float32), (heads_dev, state_dim, state_dim)
    )
    transition = eye_batch
    offset = jnp.zeros((heads_dev, state_dim, state_dim), jnp.float32)
    for span_begin in range(0, tokens_dev, SPAN):
        span_stop = span_begin + SPAN
        prev_doc = doc_index(positions[span_begin : span_begin + 1] - 1, doc_ends)[0]
        terms = span_terms(
            query_rows[:, span_begin:span_stop],
            key_rows[:, span_begin:span_stop],
            value_rows[:, span_begin:span_stop],
            decay_rows[:, span_begin:span_stop],
            strength[:, span_begin:span_stop],
            doc_ids[span_begin:span_stop],
            prev_doc,
        )
        span_list.append(terms)
        offset = apply_map(terms[5], terms[6], offset)
        transition = jnp.einsum("hcd,hde->hce", terms[5], transition, precision=top_value)

    longest = 3 * tokens_dev * ctx_count // 8
    hops = min(ctx_count - 1, -(-(longest - 1) // tokens_dev))
    inbound_state = jnp.zeros_like(offset)
    for hop in range(hops):
        outgoing = offset if hop == 0 else apply_map(transition, offset, inbound_state)
        inbound_state = from_behind(outgoing.astype(jnp.bfloat16), "ctx", 1).astype(jnp.float32)
    pieces = []
    state_now = inbound_state
    for span_number, terms in enumerate(span_list):
        pieces.append(span_output(terms, state_now))
        if span_number + 1 < len(span_list):
            state_now = apply_map(terms[5], terms[6], state_now)
    kda_out = (
        jnp.transpose(jnp.concatenate(pieces, axis=1), (1, 0, 2))
        .reshape(1, tokens_dev, heads_dev * state_dim)
        .astype(jnp.bfloat16)
    )
    width = latents.shape[2]
    lat_dim = value_up.shape[1]
    score_scale = 1.0 / math.sqrt(NOPE + ROPE)
    query_flat = mla_query[0].reshape(tokens_dev * heads_dev, width)
    row_pos = jnp.repeat(positions, heads_dev)
    row_doc = jnp.repeat(doc_ids, heads_dev)
    row_total_count = tokens_dev * heads_dev
    row_peak = jnp.full((row_total_count,), masked_score, jnp.float32)
    block_rows = lax.all_gather(latents, "ctx", axis=1, tiled=True)[0]
    row_count = block_rows.shape[0]
    key_pos = jnp.arange(row_count, dtype=jnp.int32)
    key_doc = doc_index(key_pos, doc_ends)
    scores = (
        lax.dot_general(
            query_flat, block_rows, (((1,), (1,)), ((), ())), preferred_element_type=jnp.float32
        )
        * score_scale
    )
    allowed = (
        (key_pos[None, :] <= row_pos[:, None])
        & (key_pos[None, :] >= 0)
        & (key_doc[None, :] == row_doc[:, None])
    )
    new_peak = jnp.maximum(row_peak, jnp.max(jnp.where(allowed, scores, masked_score), axis=1))
    exponent = jnp.where(allowed, jnp.exp(scores - new_peak[:, None]), 0.0)
    row_total = jnp.sum(exponent, axis=1)
    weighted = jnp.dot(
        exponent.astype(jnp.bfloat16), block_rows[:, :lat_dim], preferred_element_type=jnp.float32
    )
    row_peak, row_total, weighted = (new_peak, row_total, weighted)
    context = (
        (weighted / row_total[:, None]).astype(jnp.bfloat16).reshape(tokens_dev, heads_dev, lat_dim)
    )
    head_out = jnp.einsum(
        "thl,hlv->thv", context, value_up, preferred_element_type=jnp.float32
    ).astype(jnp.bfloat16)
    head_out = head_out.reshape(tokens_dev, heads_dev * value_up.shape[2])
    mixed = lax.psum_scatter(
        jnp.dot(head_out, out_proj, preferred_element_type=jnp.float32).astype(jnp.bfloat16),
        "head",
        scatter_dimension=0,
        tiled=True,
    )
    return (kda_out, mixed[None])


def solution(mesh):
    placed = (
        P(("group", "req"), "ctx", "head"),
        P(("group", "req"), "ctx", "head"),
        P(("group", "req"), "ctx", "head"),
        P(("group", "req"), "ctx", "head"),
        P(("group", "req"), "head", "ctx"),
        P(("group", "req"), "ctx", "head"),
        P(("group", "req"), "ctx", None),
        P("head", None, None),
        P("head", None),
        P(("group", "req"), None),
    )
    return jax.shard_map(
        local,
        mesh=mesh,
        in_specs=placed,
        out_specs=(P(("group", "req"), "ctx", "head"), P(("group", "req"), ("ctx", "head"), None)),
        check_vma=False,
    )
```

```python
import functools
import math

import jax
import jax.numpy as jnp
from jax import lax
from jax.experimental import pallas as pl
from jax.experimental.pallas import tpu as pltpu
from jax.sharding import PartitionSpec as P

ROPE = 64
NOPE = 128
SPAN = 64
HEADS_STEP = 4

masked_score = -1e30
ROWS = (((1,), (0,)), ((), ()))
TRANS = (((1,), (1,)), ((), ()))
OVER = (((0,), (0,)), ((), ()))


def from_behind(value, axis, by):
    peers = lax.axis_size(axis)
    pairs = [(i, i + by) for i in range(peers) if 0 <= i + by < peers]
    return lax.ppermute(value, axis, pairs)


def doc_index(position_list, doc_ends):
    return jnp.sum((doc_ends[None, :] <= position_list[:, None]).astype(jnp.int32), axis=1)


def dot_once(left, right, dims):
    return lax.dot_general(
        left.astype(jnp.bfloat16),
        right.astype(jnp.bfloat16),
        dims,
        preferred_element_type=jnp.float32,
    )


def halves(value):
    high = value.astype(jnp.bfloat16)
    return high, (value - high.astype(jnp.float32)).astype(jnp.bfloat16)


def dot_split(left, right, dims):
    left_high, left_low = halves(left)
    right_high, right_low = halves(right)
    return (
        dot_once(left_high, right_low, dims) + dot_once(left_low, right_high, dims)
    ) + dot_once(left_high, right_high, dims)


def delta_terms(
    query_ref,
    key_ref,
    value_ref,
    decay_ref,
    strength_ref,
    doc_col_ref,
    doc_row_ref,
    carried_ref,
    readout_ref,
    local_ref,
    transition_ref,
    offset_ref,
):
    tokens = query_ref.shape[1]
    state_dim = transition_ref.shape[1]
    spans = tokens // SPAN
    heads = range(strength_ref.shape[2])
    row = lax.broadcasted_iota(jnp.int32, (tokens, tokens), 0)
    col = lax.broadcasted_iota(jnp.int32, (tokens, tokens), 1)
    inclusive = jnp.where(row >= col, 1.0, 0.0).astype(jnp.bfloat16)
    same_doc = doc_col_ref[...] == doc_row_ref[...]
    strict = same_doc & (row > col)
    up_to = same_doc & (row >= col)
    carried = carried_ref[:, 0:1]
    tail = jnp.where(doc_col_ref[...] == doc_col_ref[tokens - 1 : tokens, :], 1.0, 0.0)
    small_row = lax.broadcasted_iota(jnp.int32, (SPAN, SPAN), 0)
    small_col = lax.broadcasted_iota(jnp.int32, (SPAN, SPAN), 1)
    queries, keys, strengths, summed = [], [], [], []
    for h in heads:
        lanes = slice(h * state_dim, (h + 1) * state_dim)
        query = query_ref[0, :, lanes].astype(jnp.float32)
        key = key_ref[0, :, lanes].astype(jnp.float32)
        queries.append(query * lax.rsqrt(jnp.sum(query * query, axis=1, keepdims=True) + 1e-06))
        keys.append(key * lax.rsqrt(jnp.sum(key * key, axis=1, keepdims=True) + 1e-06))
        strengths.append(strength_ref[0, :, h : h + 1])
        summed.append(dot_once(inclusive, decay_ref[0, :, lanes], ROWS))
    attends, lowers = [], []
    for h in heads:
        attend_rows, lower_rows = [], []
        for a in range(spans):
            here = slice(a * SPAN, (a + 1) * SPAN)
            seen = (a + 1) * SPAN
            if a == 0:
                start = jnp.zeros((1, state_dim), jnp.float32)
            else:
                start = summed[h][a * SPAN - 1 : a * SPAN]
            fall = jnp.exp(summed[h][here] - start)
            stacked = jnp.concatenate([keys[h][here] * fall, queries[h][here] * fall], axis=0)
            lifted = keys[h][:seen] * jnp.exp(start - summed[h][:seen])
            both = dot_split(stacked, lifted, TRANS)
            lower_rows.append(
                jnp.where(strict[here, :seen], both[:SPAN] * strengths[h][here], 0.0)
            )
            attend_rows.append(jnp.where(up_to[here, :seen], both[SPAN:], 0.0))
        attends.append(attend_rows)
        lowers.append(lower_rows)
    inverses = [[None] * spans for _ in heads]
    width = 1
    while width < SPAN:
        corner = (small_row // (2 * width) == small_col // (2 * width)) & (
            small_row // width > small_col // width
        )
        cells = [(h, a) for h in heads for a in range(spans)]
        parts = {
            (h, a): jnp.where(corner, lowers[h][a][:, a * SPAN :], 0.0) for h, a in cells
        }
        if width == 1:
            for h, a in cells:
                inverses[h][a] = -parts[h, a]
        else:
            lefts = {
                (h, a): parts[h, a] + dot_once(inverses[h][a], parts[h, a], ROWS)
                for h, a in cells
            }
            for h, a in cells:
                inverses[h][a] = inverses[h][a] - (
                    lefts[h, a] + dot_once(lefts[h, a], inverses[h][a], ROWS)
                )
        width *= 2
    solved = [[] for _ in heads]
    growths = [jnp.exp(summed[h]) for h in heads]
    for a in range(spans):
        here = slice(a * SPAN, (a + 1) * SPAN)
        for h in heads:
            lanes = slice(h * state_dim, (h + 1) * state_dim)
            right = strengths[h][here] * jnp.concatenate(
                [
                    carried[here] * keys[h][here] * growths[h][here],
                    value_ref[0, here, lanes].astype(jnp.float32),
                ],
                axis=1,
            )
            if a > 0:
                before = jnp.concatenate(solved[h], axis=0) if a > 1 else solved[h][0]
                right = right - dot_once(lowers[h][a][:, : a * SPAN], before, ROWS)
            solved[h].append(right + dot_once(inverses[h][a], right, ROWS))
    eye = jnp.where(
        lax.broadcasted_iota(jnp.int32, (state_dim, state_dim), 0)
        == lax.broadcasted_iota(jnp.int32, (state_dim, state_dim), 1),
        1.0,
        0.0,
    )
    for h in heads:
        lanes = slice(h * state_dim, (h + 1) * state_dim)
        whole = jnp.concatenate(solved[h], axis=0)
        whole_halves = halves(whole)
        for a in range(spans):
            here = slice(a * SPAN, (a + 1) * SPAN)
            seen = (a + 1) * SPAN
            attend_high, attend_low = halves(attends[h][a])
            read = (
                dot_once(attend_high, whole_halves[1][:seen], ROWS)
                + dot_once(attend_low, whole_halves[0][:seen], ROWS)
            ) + dot_once(attend_high, whole_halves[0][:seen], ROWS)
            readout_ref[here, lanes] = (
                carried[here] * queries[h][here] * growths[h][here] - read[:, :state_dim]
            ).astype(readout_ref.dtype)
            local_ref[here, lanes] = read[:, state_dim:]
        last = summed[h][tokens - 1 : tokens]
        key_decay = keys[h] * jnp.exp(last - summed[h]) * tail
        moved = dot_split(key_decay, whole, OVER)
        kept = carried[tokens - 1 : tokens] * growths[h][tokens - 1 : tokens]
        transition_ref[h] = (eye * kept - moved[:, :state_dim]).astype(transition_ref.dtype)
        offset_ref[h] = moved[:, state_dim:]


def delta_readout(readout_ref, local_ref, state_ref, out_ref):
    state_dim = state_ref.shape[1]
    for h in range(state_ref.shape[0]):
        lanes = slice(h * state_dim, (h + 1) * state_dim)
        out_ref[0, :, lanes] = (
            local_ref[:, lanes]
            + jnp.dot(readout_ref[:, lanes], state_ref[h], preferred_element_type=jnp.float32)
        ).astype(out_ref.dtype)


def local(
    kda_query,
    kda_key,
    kda_value,
    log_decay,
    write_strength,
    mla_query,
    latents,
    value_up,
    out_proj,
    doc_lengths,
):
    tokens_dev = kda_query.shape[1]
    heads_dev = write_strength.shape[1]
    state_dim = kda_query.shape[2] // heads_dev
    ctx_count = lax.axis_size("ctx")
    ctx_place = lax.axis_index("ctx")
    longest = 3 * tokens_dev * ctx_count // 8
    hops = min(ctx_count - 1, -(-(longest - 1) // tokens_dev))
    first_pos = ctx_place * tokens_dev
    positions = first_pos + jnp.arange(tokens_dev, dtype=jnp.int32)
    doc_ends = jnp.cumsum(doc_lengths[0])
    doc_ids = doc_index(positions, doc_ends)
    prev_doc = doc_index(first_pos[None] - 1, doc_ends)
    carried = (doc_ids == prev_doc).astype(jnp.float32)

    window = [from_behind(latents[0], "ctx", by) for by in range(hops, 0, -1)]
    block_rows = jnp.concatenate(window + [latents[0]], axis=0)

    steps = heads_dev // HEADS_STEP
    lanes_step = HEADS_STEP * state_dim
    strength = jnp.transpose(
        write_strength[0].reshape(steps, HEADS_STEP, tokens_dev), (0, 2, 1)
    )
    packed = pl.BlockSpec((1, tokens_dev, lanes_step), lambda i: (0, 0, i))
    flat = pl.BlockSpec((tokens_dev, lanes_step), lambda i: (0, i))
    column = pl.BlockSpec((tokens_dev, 1), lambda i: (0, 0))
    square = pl.BlockSpec((HEADS_STEP, state_dim, state_dim), lambda i: (i, 0, 0))
    readout, local_part, transition, offset = pl.pallas_call(
        delta_terms,
        grid=(steps,),
        in_specs=[packed] * 4
        + [
            pl.BlockSpec((1, tokens_dev, HEADS_STEP), lambda i: (i, 0, 0)),
            column,
            pl.BlockSpec((1, tokens_dev), lambda i: (0, 0)),
            column,
        ],
        out_specs=[flat, flat, square, square],
        out_shape=[
            jax.ShapeDtypeStruct((tokens_dev, heads_dev * state_dim), jnp.bfloat16),
            jax.ShapeDtypeStruct((tokens_dev, heads_dev * state_dim), jnp.float32),
            jax.ShapeDtypeStruct((heads_dev, state_dim, state_dim), jnp.bfloat16),
            jax.ShapeDtypeStruct((heads_dev, state_dim, state_dim), jnp.float32),
        ],
        compiler_params=pltpu.CompilerParams(vmem_limit_bytes=48 << 20),
        cost_estimate=pl.CostEstimate(
            flops=20_000_000_000, bytes_accessed=8_000_000, transcendentals=0
        ),
    )(
        kda_query,
        kda_key,
        kda_value,
        log_decay,
        strength,
        doc_ids[:, None],
        doc_ids[None, :],
        carried[:, None],
    )

    inbound_state = None
    for hop in range(hops):
        outgoing = offset
        if hop > 0:
            outgoing = offset + jnp.einsum(
                "hcd,hdv->hcv", transition, inbound_state, preferred_element_type=jnp.float32
            )
        inbound_state = from_behind(outgoing.astype(jnp.bfloat16), "ctx", 1)
    kda_out = pl.pallas_call(
        delta_readout,
        grid=(steps,),
        in_specs=[flat, flat, square],
        out_specs=packed,
        out_shape=jax.ShapeDtypeStruct((1, tokens_dev, heads_dev * state_dim), jnp.bfloat16),
        cost_estimate=pl.CostEstimate(
            flops=100_000_000, bytes_accessed=4_000_000, transcendentals=0
        ),
    )(readout, local_part, inbound_state)

    width = latents.shape[2]
    lat_dim = value_up.shape[1]
    score_scale = 1.0 / math.sqrt(NOPE + ROPE)
    query_flat = mla_query[0].reshape(tokens_dev * heads_dev, width)
    row_pos = jnp.repeat(positions, heads_dev)
    row_doc = jnp.repeat(doc_ids, heads_dev)
    row_total_count = tokens_dev * heads_dev
    row_peak = jnp.full((row_total_count,), masked_score, jnp.float32)
    row_count = block_rows.shape[0]
    key_pos = first_pos - hops * tokens_dev + jnp.arange(row_count, dtype=jnp.int32)
    key_doc = doc_index(key_pos, doc_ends)
    scores = (
        lax.dot_general(
            query_flat, block_rows, (((1,), (1,)), ((), ())), preferred_element_type=jnp.float32
        )
        * score_scale
    )
    allowed = (
        (key_pos[None, :] <= row_pos[:, None])
        & (key_pos[None, :] >= 0)
        & (key_doc[None, :] == row_doc[:, None])
    )
    new_peak = jnp.maximum(row_peak, jnp.max(jnp.where(allowed, scores, masked_score), axis=1))
    exponent = jnp.where(allowed, jnp.exp(scores - new_peak[:, None]), 0.0)
    row_total = jnp.sum(exponent, axis=1)
    weighted = jnp.dot(
        exponent.astype(jnp.bfloat16), block_rows[:, :lat_dim], preferred_element_type=jnp.float32
    )
    row_peak, row_total, weighted = (new_peak, row_total, weighted)
    context = (
        (weighted / row_total[:, None]).astype(jnp.bfloat16).reshape(tokens_dev, heads_dev, lat_dim)
    )
    head_out = jnp.einsum(
        "thl,hlv->thv", context, value_up, preferred_element_type=jnp.float32
    ).astype(jnp.bfloat16)
    head_out = head_out.reshape(tokens_dev, heads_dev * value_up.shape[2])
    mixed = lax.psum_scatter(
        jnp.dot(head_out, out_proj, preferred_element_type=jnp.float32).astype(jnp.bfloat16),
        "head",
        scatter_dimension=0,
        tiled=True,
    )
    return (kda_out, mixed[None])


def solution(mesh):
    placed = (
        P(("group", "req"), "ctx", "head"),
        P(("group", "req"), "ctx", "head"),
        P(("group", "req"), "ctx", "head"),
        P(("group", "req"), "ctx", "head"),
        P(("group", "req"), "head", "ctx"),
        P(("group", "req"), "ctx", "head"),
        P(("group", "req"), "ctx", None),
        P("head", None, None),
        P("head", None),
        P(("group", "req"), None),
    )
    return jax.shard_map(
        local,
        mesh=mesh,
        in_specs=placed,
        out_specs=(P(("group", "req"), "ctx", "head"), P(("group", "req"), ("ctx", "head"), None)),
        check_vma=False,
    )
```

```python
import functools
import math

import jax
import jax.numpy as jnp
from jax import lax
from jax.experimental import pallas as pl
from jax.experimental.pallas import tpu as pltpu
from jax.sharding import PartitionSpec as P

ROPE = 64
NOPE = 128
SPAN = 64
HEADS_STEP = 4

masked_score = -1e30
ROWS = (((1,), (0,)), ((), ()))
TRANS = (((1,), (1,)), ((), ()))
OVER = (((0,), (0,)), ((), ()))


def from_behind(value, axis, by):
    peers = lax.axis_size(axis)
    pairs = [(i, i + by) for i in range(peers) if 0 <= i + by < peers]
    return lax.ppermute(value, axis, pairs)


def doc_index(position_list, doc_ends):
    return jnp.sum((doc_ends[None, :] <= position_list[:, None]).astype(jnp.int32), axis=1)


def dot_once(left, right, dims):
    return lax.dot_general(
        left.astype(jnp.bfloat16),
        right.astype(jnp.bfloat16),
        dims,
        preferred_element_type=jnp.float32,
    )


def halves(value):
    high = value.astype(jnp.bfloat16)
    return high, (value - high.astype(jnp.float32)).astype(jnp.bfloat16)


def dot_split(left, right, dims):
    left_high, left_low = halves(left)
    right_high, right_low = halves(right)
    return (
        dot_once(left_high, right_low, dims) + dot_once(left_low, right_high, dims)
    ) + dot_once(left_high, right_high, dims)


def delta_terms(
    query_ref,
    key_ref,
    value_ref,
    decay_ref,
    strength_ref,
    doc_col_ref,
    doc_row_ref,
    carried_ref,
    readout_ref,
    local_ref,
    transition_ref,
    offset_ref,
):
    tokens = query_ref.shape[1]
    state_dim = transition_ref.shape[1]
    spans = tokens // SPAN
    heads = range(strength_ref.shape[2])
    row = lax.broadcasted_iota(jnp.int32, (tokens, tokens), 0)
    col = lax.broadcasted_iota(jnp.int32, (tokens, tokens), 1)
    inclusive = jnp.where(row >= col, 1.0, 0.0).astype(jnp.bfloat16)
    same_doc = doc_col_ref[...] == doc_row_ref[...]
    strict = same_doc & (row > col)
    up_to = same_doc & (row >= col)
    carried = carried_ref[:, 0:1]
    tail = jnp.where(doc_col_ref[...] == doc_col_ref[tokens - 1 : tokens, :], 1.0, 0.0)
    small_row = lax.broadcasted_iota(jnp.int32, (SPAN, SPAN), 0)
    small_col = lax.broadcasted_iota(jnp.int32, (SPAN, SPAN), 1)
    queries, keys, strengths, summed = [], [], [], []
    for h in heads:
        lanes = slice(h * state_dim, (h + 1) * state_dim)
        query = query_ref[0, :, lanes].astype(jnp.float32)
        key = key_ref[0, :, lanes].astype(jnp.float32)
        queries.append(query * lax.rsqrt(jnp.sum(query * query, axis=1, keepdims=True) + 1e-06))
        keys.append(key * lax.rsqrt(jnp.sum(key * key, axis=1, keepdims=True) + 1e-06))
        strengths.append(strength_ref[0, :, h : h + 1])
        summed.append(dot_once(inclusive, decay_ref[0, :, lanes], ROWS))
    attends, lowers = [], []
    for h in heads:
        attend_rows, lower_rows = [], []
        for a in range(spans):
            here = slice(a * SPAN, (a + 1) * SPAN)
            seen = (a + 1) * SPAN
            if a == 0:
                start = jnp.zeros((1, state_dim), jnp.float32)
            else:
                start = summed[h][a * SPAN - 1 : a * SPAN]
            fall = jnp.exp(summed[h][here] - start)
            stacked = jnp.concatenate([keys[h][here] * fall, queries[h][here] * fall], axis=0)
            lifted = keys[h][:seen] * jnp.exp(start - summed[h][:seen])
            both = dot_split(stacked, lifted, TRANS)
            lower_rows.append(
                jnp.where(strict[here, :seen], both[:SPAN] * strengths[h][here], 0.0)
            )
            attend_rows.append(jnp.where(up_to[here, :seen], both[SPAN:], 0.0))
        attends.append(attend_rows)
        lowers.append(lower_rows)
    inverses = [[None] * spans for _ in heads]
    width = 1
    while width < SPAN:
        corner = (small_row // (2 * width) == small_col // (2 * width)) & (
            small_row // width > small_col // width
        )
        cells = [(h, a) for h in heads for a in range(spans)]
        parts = {
            (h, a): jnp.where(corner, lowers[h][a][:, a * SPAN :], 0.0) for h, a in cells
        }
        if width == 1:
            for h, a in cells:
                inverses[h][a] = -parts[h, a]
        else:
            lefts = {
                (h, a): parts[h, a] + dot_once(inverses[h][a], parts[h, a], ROWS)
                for h, a in cells
            }
            for h, a in cells:
                inverses[h][a] = inverses[h][a] - (
                    lefts[h, a] + dot_once(lefts[h, a], inverses[h][a], ROWS)
                )
        width *= 2
    solved = [[] for _ in heads]
    growths = [jnp.exp(summed[h]) for h in heads]
    for a in range(spans):
        here = slice(a * SPAN, (a + 1) * SPAN)
        for h in heads:
            lanes = slice(h * state_dim, (h + 1) * state_dim)
            right = strengths[h][here] * jnp.concatenate(
                [
                    carried[here] * keys[h][here] * growths[h][here],
                    value_ref[0, here, lanes].astype(jnp.float32),
                ],
                axis=1,
            )
            if a > 0:
                before = jnp.concatenate(solved[h], axis=0) if a > 1 else solved[h][0]
                right = right - dot_once(lowers[h][a][:, : a * SPAN], before, ROWS)
            solved[h].append(right + dot_once(inverses[h][a], right, ROWS))
    eye = jnp.where(
        lax.broadcasted_iota(jnp.int32, (state_dim, state_dim), 0)
        == lax.broadcasted_iota(jnp.int32, (state_dim, state_dim), 1),
        1.0,
        0.0,
    )
    for h in heads:
        lanes = slice(h * state_dim, (h + 1) * state_dim)
        whole = jnp.concatenate(solved[h], axis=0)
        whole_halves = halves(whole)
        for a in range(spans):
            here = slice(a * SPAN, (a + 1) * SPAN)
            seen = (a + 1) * SPAN
            attend_high, attend_low = halves(attends[h][a])
            read = (
                dot_once(attend_high, whole_halves[1][:seen], ROWS)
                + dot_once(attend_low, whole_halves[0][:seen], ROWS)
            ) + dot_once(attend_high, whole_halves[0][:seen], ROWS)
            readout_ref[here, lanes] = (
                carried[here] * queries[h][here] * growths[h][here] - read[:, :state_dim]
            ).astype(readout_ref.dtype)
            local_ref[here, lanes] = read[:, state_dim:]
        last = summed[h][tokens - 1 : tokens]
        key_decay = keys[h] * jnp.exp(last - summed[h]) * tail
        moved = dot_split(key_decay, whole, OVER)
        kept = carried[tokens - 1 : tokens] * growths[h][tokens - 1 : tokens]
        transition_ref[h] = (eye * kept - moved[:, :state_dim]).astype(transition_ref.dtype)
        offset_ref[h] = moved[:, state_dim:]


def delta_readout(readout_ref, local_ref, state_ref, out_ref):
    state_dim = state_ref.shape[1]
    for h in range(state_ref.shape[0]):
        lanes = slice(h * state_dim, (h + 1) * state_dim)
        out_ref[0, :, lanes] = (
            local_ref[:, lanes]
            + jnp.dot(readout_ref[:, lanes], state_ref[h], preferred_element_type=jnp.float32)
        ).astype(out_ref.dtype)


def latent_attention(
    place_ref,
    query_ref,
    even_ref,
    odd_ref,
    bias_ref,
    up_ref,
    proj_ref,
    out_ref,
    total_ref,
    *,
    width,
    score_scale,
):
    rows = query_ref.shape[1]
    lat_dim = up_ref.shape[1]
    pairs = up_ref.shape[0] // 2
    wide = even_ref.shape[1]
    bias = bias_ref[...]
    bias = jnp.concatenate([bias] * pairs, axis=0) if pairs > 1 else bias
    contexts = []
    for key_ref, skip in ((even_ref, 0), (odd_ref, 2 * width - wide)):
        stacked = [
            query_ref[0, :, 2 * p * width + skip : 2 * p * width + skip + wide]
            for p in range(pairs)
        ]
        query = jnp.concatenate(stacked, axis=0) if pairs > 1 else stacked[0]
        scores = lax.dot_general(
            query, key_ref[...], TRANS, preferred_element_type=jnp.float32
        )
        scores = scores * score_scale + bias
        exponent = jnp.exp(scores - jnp.max(scores, axis=1, keepdims=True))
        row_total = jnp.sum(exponent, axis=1, keepdims=True)
        weighted = jnp.dot(
            exponent.astype(jnp.bfloat16),
            even_ref[:, :lat_dim],
            preferred_element_type=jnp.float32,
        )
        contexts.append((weighted / row_total).astype(jnp.bfloat16))
    head_out = []
    for p in range(pairs):
        for parity in range(2):
            head_out.append(
                jnp.dot(
                    contexts[parity][p * rows : (p + 1) * rows],
                    up_ref[2 * p + parity],
                    preferred_element_type=jnp.float32,
                ).astype(jnp.bfloat16)
            )
    part = jnp.dot(
        jnp.concatenate(head_out, axis=1), proj_ref[...], preferred_element_type=jnp.float32
    )
    step = pl.program_id(0)

    @pl.when(step == 0)
    def _():
        total_ref[...] = part

    @pl.when(step > 0)
    def _():
        total_ref[...] += part

    @pl.when(step == pl.num_programs(0) - 1)
    def _():
        out_ref[...] = total_ref[...].astype(out_ref.dtype)


def local(
    kda_query,
    kda_key,
    kda_value,
    log_decay,
    write_strength,
    mla_query,
    latents,
    value_up,
    out_proj,
    doc_lengths,
):
    tokens_dev = kda_query.shape[1]
    heads_dev = write_strength.shape[1]
    state_dim = kda_query.shape[2] // heads_dev
    ctx_count = lax.axis_size("ctx")
    ctx_place = lax.axis_index("ctx")
    longest = 3 * tokens_dev * ctx_count // 8
    hops = min(ctx_count - 1, -(-(longest - 1) // tokens_dev))
    first_pos = ctx_place * tokens_dev
    positions = first_pos + jnp.arange(tokens_dev, dtype=jnp.int32)
    doc_ends = jnp.cumsum(doc_lengths[0])
    doc_ids = doc_index(positions, doc_ends)
    prev_doc = doc_index(first_pos[None] - 1, doc_ends)
    carried = (doc_ids == prev_doc).astype(jnp.float32)

    window = [from_behind(latents[0], "ctx", by) for by in range(hops, 0, -1)]
    block_rows = jnp.concatenate(window + [latents[0]], axis=0)

    steps = heads_dev // HEADS_STEP
    lanes_step = HEADS_STEP * state_dim
    strength = jnp.transpose(
        write_strength[0].reshape(steps, HEADS_STEP, tokens_dev), (0, 2, 1)
    )
    packed = pl.BlockSpec((1, tokens_dev, lanes_step), lambda i: (0, 0, i))
    flat = pl.BlockSpec((tokens_dev, lanes_step), lambda i: (0, i))
    column = pl.BlockSpec((tokens_dev, 1), lambda i: (0, 0))
    square = pl.BlockSpec((HEADS_STEP, state_dim, state_dim), lambda i: (i, 0, 0))
    readout, local_part, transition, offset = pl.pallas_call(
        delta_terms,
        grid=(steps,),
        in_specs=[packed] * 4
        + [
            pl.BlockSpec((1, tokens_dev, HEADS_STEP), lambda i: (i, 0, 0)),
            column,
            pl.BlockSpec((1, tokens_dev), lambda i: (0, 0)),
            column,
        ],
        out_specs=[flat, flat, square, square],
        out_shape=[
            jax.ShapeDtypeStruct((tokens_dev, heads_dev * state_dim), jnp.bfloat16),
            jax.ShapeDtypeStruct((tokens_dev, heads_dev * state_dim), jnp.float32),
            jax.ShapeDtypeStruct((heads_dev, state_dim, state_dim), jnp.bfloat16),
            jax.ShapeDtypeStruct((heads_dev, state_dim, state_dim), jnp.float32),
        ],
        compiler_params=pltpu.CompilerParams(vmem_limit_bytes=48 << 20),
        cost_estimate=pl.CostEstimate(
            flops=20_000_000_000, bytes_accessed=8_000_000, transcendentals=0
        ),
    )(
        kda_query,
        kda_key,
        kda_value,
        log_decay,
        strength,
        doc_ids[:, None],
        doc_ids[None, :],
        carried[:, None],
    )

    width = latents.shape[2]
    vhead = value_up.shape[2]
    model = out_proj.shape[1]
    row_count = block_rows.shape[0]
    key_pos = first_pos - hops * tokens_dev + jnp.arange(row_count, dtype=jnp.int32)
    key_doc = doc_index(key_pos, doc_ends)
    allowed = (
        (key_pos[None, :] <= positions[:, None])
        & (key_pos[None, :] >= 0)
        & (key_doc[None, :] == doc_ids[:, None])
    )
    bias = jnp.where(allowed, 0.0, masked_score)
    spare = -width % 128
    even_rows = jnp.pad(block_rows, ((0, 0), (0, spare)))
    odd_rows = jnp.pad(block_rows, ((0, 0), (spare, 0)))
    rows = tokens_dev // 2

    def attention(place, dtype):
        keys = pl.BlockSpec((row_count, width + spare), lambda i, at: (0, 0))
        return pl.pallas_call(
            functools.partial(
                latent_attention, width=width, score_scale=1.0 / math.sqrt(NOPE + ROPE)
            ),
            grid_spec=pltpu.PrefetchScalarGridSpec(
                num_scalar_prefetch=1,
                grid=(steps,),
                in_specs=[
                    pl.BlockSpec((1, rows, HEADS_STEP * width), lambda i, at: (0, at[0], i)),
                    keys,
                    keys,
                    pl.BlockSpec((rows, row_count), lambda i, at: (at[0], 0)),
                    pl.BlockSpec((HEADS_STEP,) + value_up.shape[1:], lambda i, at: (i, 0, 0)),
                    pl.BlockSpec((HEADS_STEP * vhead, model), lambda i, at: (i, 0)),
                ],
                out_specs=pl.BlockSpec((rows, model), lambda i, at: (0, 0)),
                scratch_shapes=[pltpu.VMEM((rows, model), jnp.float32)],
            ),
            out_shape=jax.ShapeDtypeStruct((rows, model), dtype),
            compiler_params=pltpu.CompilerParams(vmem_limit_bytes=48 << 20),
            cost_estimate=pl.CostEstimate(
                flops=12_000_000_000, bytes_accessed=16_000_000, transcendentals=0
            ),
        )(place, mla_query, even_rows, odd_rows, bias, value_up, out_proj)

    def relayed(inbound_state, hop):
        outgoing = offset
        if hop > 0:
            outgoing = offset + jnp.einsum(
                "hcd,hdv->hcv", transition, inbound_state, preferred_element_type=jnp.float32
            )
        return outgoing.astype(jnp.bfloat16)

    head_count = lax.axis_size("head")
    mine = lax.axis_index("head") if head_count == 2 else jnp.int32(1)
    first, outgoing = lax.optimization_barrier(((1 - mine)[None], relayed(None, 0)))
    inbound_state = from_behind(outgoing, "ctx", 1)
    far_part = attention(first, jnp.bfloat16)
    if head_count == 2:
        far_part = lax.ppermute(far_part, "head", [(0, 1), (1, 0)])
    second = mine[None]
    for hop in range(1, hops):
        outgoing = relayed(inbound_state, hop)
        second, outgoing = lax.optimization_barrier((second, outgoing))
        inbound_state = from_behind(outgoing, "ctx", 1)
    if head_count == 2:
        near_part = attention(second, jnp.float32)
        mixed = (near_part + far_part.astype(jnp.float32)).astype(jnp.bfloat16)
    else:
        near_part = attention(second, jnp.bfloat16)
        mixed = lax.psum_scatter(
            jnp.concatenate([far_part, near_part], axis=0),
            "head",
            scatter_dimension=0,
            tiled=True,
        )
    kda_out = pl.pallas_call(
        delta_readout,
        grid=(steps,),
        in_specs=[flat, flat, square],
        out_specs=packed,
        out_shape=jax.ShapeDtypeStruct((1, tokens_dev, heads_dev * state_dim), jnp.bfloat16),
        cost_estimate=pl.CostEstimate(
            flops=100_000_000, bytes_accessed=4_000_000, transcendentals=0
        ),
    )(readout, local_part, inbound_state)
    return (kda_out, mixed[None])


def solution(mesh):
    placed = (
        P(("group", "req"), "ctx", "head"),
        P(("group", "req"), "ctx", "head"),
        P(("group", "req"), "ctx", "head"),
        P(("group", "req"), "ctx", "head"),
        P(("group", "req"), "head", "ctx"),
        P(("group", "req"), "ctx", "head"),
        P(("group", "req"), "ctx", None),
        P("head", None, None),
        P("head", None),
        P(("group", "req"), None),
    )
    return jax.shard_map(
        local,
        mesh=mesh,
        in_specs=placed,
        out_specs=(P(("group", "req"), "ctx", "head"), P(("group", "req"), ("ctx", "head"), None)),
        check_vma=False,
    )
```

```python
import functools
import math

import jax
import jax.numpy as jnp
from jax import lax
from jax.experimental import pallas as pl
from jax.experimental.pallas import tpu as pltpu
from jax.sharding import PartitionSpec as P

ROPE = 64
NOPE = 128
SPAN = 64
HEADS_STEP = 4

masked_score = -1e30
ROWS = (((1,), (0,)), ((), ()))
TRANS = (((1,), (1,)), ((), ()))
OVER = (((0,), (0,)), ((), ()))


def from_behind(value, axis, by):
    peers = lax.axis_size(axis)
    pairs = [(i, i + by) for i in range(peers) if 0 <= i + by < peers]
    return lax.ppermute(value, axis, pairs)


def in_place(value):
    return pltpu.with_memory_space_constraint(value, pltpu.HBM)


def doc_index(position_list, doc_ends):
    return jnp.sum((doc_ends[None, :] <= position_list[:, None]).astype(jnp.int32), axis=1)


def dot_once(left, right, dims):
    return lax.dot_general(
        left.astype(jnp.bfloat16),
        right.astype(jnp.bfloat16),
        dims,
        preferred_element_type=jnp.float32,
    )


def halves(value):
    high = value.astype(jnp.bfloat16)
    return high, (value - high.astype(jnp.float32)).astype(jnp.bfloat16)


def dot_split(left, right, dims):
    left_high, left_low = halves(left)
    right_high, right_low = halves(right)
    return (
        dot_once(left_high, right_low, dims) + dot_once(left_low, right_high, dims)
    ) + dot_once(left_high, right_high, dims)


def delta_terms(
    query_ref,
    key_ref,
    value_ref,
    decay_ref,
    strength_ref,
    doc_col_ref,
    doc_row_ref,
    carried_ref,
    readout_ref,
    local_ref,
    transition_ref,
    offset_ref,
):
    tokens = query_ref.shape[1]
    state_dim = transition_ref.shape[1]
    spans = tokens // SPAN
    heads = range(strength_ref.shape[2])
    row = lax.broadcasted_iota(jnp.int32, (tokens, tokens), 0)
    col = lax.broadcasted_iota(jnp.int32, (tokens, tokens), 1)
    inclusive = jnp.where(row >= col, 1.0, 0.0).astype(jnp.bfloat16)
    same_doc = doc_col_ref[...] == doc_row_ref[...]
    strict = same_doc & (row > col)
    up_to = same_doc & (row >= col)
    carried = carried_ref[:, 0:1]
    tail = jnp.where(doc_col_ref[...] == doc_col_ref[tokens - 1 : tokens, :], 1.0, 0.0)
    small_row = lax.broadcasted_iota(jnp.int32, (SPAN, SPAN), 0)
    small_col = lax.broadcasted_iota(jnp.int32, (SPAN, SPAN), 1)
    queries, keys, strengths, summed = [], [], [], []
    for h in heads:
        lanes = slice(h * state_dim, (h + 1) * state_dim)
        query = query_ref[0, :, lanes].astype(jnp.float32)
        key = key_ref[0, :, lanes].astype(jnp.float32)
        queries.append(query * lax.rsqrt(jnp.sum(query * query, axis=1, keepdims=True) + 1e-06))
        keys.append(key * lax.rsqrt(jnp.sum(key * key, axis=1, keepdims=True) + 1e-06))
        strengths.append(strength_ref[0, :, h : h + 1])
        summed.append(dot_once(inclusive, decay_ref[0, :, lanes], ROWS))
    attends, lowers = [], []
    for h in heads:
        attend_rows, lower_rows = [], []
        for a in range(spans):
            here = slice(a * SPAN, (a + 1) * SPAN)
            seen = (a + 1) * SPAN
            if a == 0:
                start = jnp.zeros((1, state_dim), jnp.float32)
            else:
                start = summed[h][a * SPAN - 1 : a * SPAN]
            fall = jnp.exp(summed[h][here] - start)
            stacked = jnp.concatenate([keys[h][here] * fall, queries[h][here] * fall], axis=0)
            lifted = keys[h][:seen] * jnp.exp(start - summed[h][:seen])
            both = dot_split(stacked, lifted, TRANS)
            lower_rows.append(
                jnp.where(strict[here, :seen], both[:SPAN] * strengths[h][here], 0.0)
            )
            attend_rows.append(jnp.where(up_to[here, :seen], both[SPAN:], 0.0))
        attends.append(attend_rows)
        lowers.append(lower_rows)
    inverses = [[None] * spans for _ in heads]
    width = 1
    while width < SPAN:
        corner = (small_row // (2 * width) == small_col // (2 * width)) & (
            small_row // width > small_col // width
        )
        cells = [(h, a) for h in heads for a in range(spans)]
        parts = {
            (h, a): jnp.where(corner, lowers[h][a][:, a * SPAN :], 0.0) for h, a in cells
        }
        if width == 1:
            for h, a in cells:
                inverses[h][a] = -parts[h, a]
        else:
            lefts = {
                (h, a): parts[h, a] + dot_once(inverses[h][a], parts[h, a], ROWS)
                for h, a in cells
            }
            for h, a in cells:
                inverses[h][a] = inverses[h][a] - (
                    lefts[h, a] + dot_once(lefts[h, a], inverses[h][a], ROWS)
                )
        width *= 2
    solved = [[] for _ in heads]
    growths = [jnp.exp(summed[h]) for h in heads]
    for a in range(spans):
        here = slice(a * SPAN, (a + 1) * SPAN)
        for h in heads:
            lanes = slice(h * state_dim, (h + 1) * state_dim)
            right = strengths[h][here] * jnp.concatenate(
                [
                    carried[here] * keys[h][here] * growths[h][here],
                    value_ref[0, here, lanes].astype(jnp.float32),
                ],
                axis=1,
            )
            if a > 0:
                before = jnp.concatenate(solved[h], axis=0) if a > 1 else solved[h][0]
                right = right - dot_once(lowers[h][a][:, : a * SPAN], before, ROWS)
            solved[h].append(right + dot_once(inverses[h][a], right, ROWS))
    eye = jnp.where(
        lax.broadcasted_iota(jnp.int32, (state_dim, state_dim), 0)
        == lax.broadcasted_iota(jnp.int32, (state_dim, state_dim), 1),
        1.0,
        0.0,
    )
    for h in heads:
        lanes = slice(h * state_dim, (h + 1) * state_dim)
        whole = jnp.concatenate(solved[h], axis=0)
        for a in range(spans):
            here = slice(a * SPAN, (a + 1) * SPAN)
            seen = (a + 1) * SPAN
            read = dot_once(attends[h][a], whole[:seen], ROWS)
            readout_ref[here, lanes] = (
                carried[here] * queries[h][here] * growths[h][here] - read[:, :state_dim]
            ).astype(readout_ref.dtype)
            local_ref[here, lanes] = read[:, state_dim:]
        last = summed[h][tokens - 1 : tokens]
        key_decay = keys[h] * jnp.exp(last - summed[h]) * tail
        moved = dot_once(key_decay, whole, OVER)
        kept = carried[tokens - 1 : tokens] * growths[h][tokens - 1 : tokens]
        transition_ref[h] = (eye * kept - moved[:, :state_dim]).astype(transition_ref.dtype)
        offset_ref[h] = moved[:, state_dim:]


def delta_readout(readout_ref, local_ref, state_ref, out_ref):
    state_dim = state_ref.shape[1]
    for h in range(state_ref.shape[0]):
        lanes = slice(h * state_dim, (h + 1) * state_dim)
        out_ref[0, :, lanes] = (
            local_ref[:, lanes]
            + jnp.dot(readout_ref[:, lanes], state_ref[h], preferred_element_type=jnp.float32)
        ).astype(out_ref.dtype)


def latent_attention(
    place_ref,
    query_ref,
    even_ref,
    odd_ref,
    bias_ref,
    up_ref,
    proj_ref,
    out_ref,
    total_ref,
    *,
    width,
    first_key,
    score_scale,
):
    rows = query_ref.shape[1]
    key_count = bias_ref.shape[2]
    keys = pl.ds(pl.multiple_of(place_ref[0] * rows + first_key, math.gcd(rows, 16)), key_count)
    lat_dim = up_ref.shape[1]
    pairs = up_ref.shape[0] // 2
    wide = even_ref.shape[1]
    bias = bias_ref[0]
    bias = jnp.concatenate([bias] * pairs, axis=0) if pairs > 1 else bias
    contexts = []
    for key_ref, skip in ((even_ref, 0), (odd_ref, 2 * width - wide)):
        stacked = [
            query_ref[0, :, 2 * p * width + skip : 2 * p * width + skip + wide]
            for p in range(pairs)
        ]
        query = jnp.concatenate(stacked, axis=0) if pairs > 1 else stacked[0]
        scores = lax.dot_general(
            query, key_ref[keys, :], TRANS, preferred_element_type=jnp.float32
        )
        scores = scores * score_scale + bias
        exponent = jnp.exp(scores - jnp.max(scores, axis=1, keepdims=True))
        row_total = jnp.sum(exponent, axis=1, keepdims=True)
        weighted = jnp.dot(
            exponent.astype(jnp.bfloat16),
            even_ref[keys, :lat_dim],
            preferred_element_type=jnp.float32,
        )
        contexts.append((weighted / row_total).astype(jnp.bfloat16))
    head_out = []
    for p in range(pairs):
        for parity in range(2):
            head_out.append(
                jnp.dot(
                    contexts[parity][p * rows : (p + 1) * rows],
                    up_ref[2 * p + parity],
                    preferred_element_type=jnp.float32,
                ).astype(jnp.bfloat16)
            )
    part = jnp.dot(
        jnp.concatenate(head_out, axis=1), proj_ref[...], preferred_element_type=jnp.float32
    )
    step = pl.program_id(0)

    @pl.when(step == 0)
    def _():
        total_ref[...] = part

    @pl.when(step > 0)
    def _():
        total_ref[...] += part

    @pl.when(step == pl.num_programs(0) - 1)
    def _():
        out_ref[...] = total_ref[...].astype(out_ref.dtype)


def local(
    kda_query,
    kda_key,
    kda_value,
    log_decay,
    write_strength,
    mla_query,
    latents,
    value_up,
    out_proj,
    doc_lengths,
):
    tokens_dev = kda_query.shape[1]
    heads_dev = write_strength.shape[1]
    state_dim = kda_query.shape[2] // heads_dev
    ctx_count = lax.axis_size("ctx")
    ctx_place = lax.axis_index("ctx")
    longest = 3 * tokens_dev * ctx_count // 8
    hops = min(ctx_count - 1, -(-(longest - 1) // tokens_dev))
    first_pos = ctx_place * tokens_dev
    positions = first_pos + jnp.arange(tokens_dev, dtype=jnp.int32)
    doc_ends = jnp.cumsum(doc_lengths[0])
    doc_ids = doc_index(positions, doc_ends)
    prev_doc = doc_index(first_pos[None] - 1, doc_ends)
    carried = (doc_ids == prev_doc).astype(jnp.float32)

    window = [from_behind(latents[0], "ctx", by) for by in range(hops, 0, -1)]
    block_rows = jnp.concatenate(window + [latents[0]], axis=0)

    steps = heads_dev // HEADS_STEP
    lanes_step = HEADS_STEP * state_dim
    strength = jnp.transpose(
        write_strength[0].reshape(steps, HEADS_STEP, tokens_dev), (0, 2, 1)
    )
    packed = pl.BlockSpec((1, tokens_dev, lanes_step), lambda i: (0, 0, i))
    flat = pl.BlockSpec((tokens_dev, lanes_step), lambda i: (0, i))
    column = pl.BlockSpec((tokens_dev, 1), lambda i: (0, 0))
    square = pl.BlockSpec((HEADS_STEP, state_dim, state_dim), lambda i: (i, 0, 0))
    readout, local_part, transition, offset = pl.pallas_call(
        delta_terms,
        grid=(steps,),
        in_specs=[packed] * 4
        + [
            pl.BlockSpec((1, tokens_dev, HEADS_STEP), lambda i: (i, 0, 0)),
            column,
            pl.BlockSpec((1, tokens_dev), lambda i: (0, 0)),
            column,
        ],
        out_specs=[flat, flat, square, square],
        out_shape=[
            jax.ShapeDtypeStruct((tokens_dev, heads_dev * state_dim), jnp.bfloat16),
            jax.ShapeDtypeStruct((tokens_dev, heads_dev * state_dim), jnp.float32),
            jax.ShapeDtypeStruct((heads_dev, state_dim, state_dim), jnp.bfloat16),
            jax.ShapeDtypeStruct((heads_dev, state_dim, state_dim), jnp.float32),
        ],
        compiler_params=pltpu.CompilerParams(vmem_limit_bytes=48 << 20),
        cost_estimate=pl.CostEstimate(
            flops=20_000_000_000, bytes_accessed=8_000_000, transcendentals=0
        ),
    )(
        in_place(kda_query),
        in_place(kda_key),
        in_place(kda_value),
        in_place(log_decay),
        strength,
        doc_ids[:, None],
        doc_ids[None, :],
        carried[:, None],
    )

    width = latents.shape[2]
    vhead = value_up.shape[2]
    model = out_proj.shape[1]
    row_count = block_rows.shape[0]
    rows = tokens_dev // 2
    back = -(-(longest - 1) // rows) * rows
    first_key = hops * tokens_dev - back
    half_pos = positions.reshape(2, rows)
    key_pos = half_pos[:, :1] - back + jnp.arange(back + rows, dtype=jnp.int32)[None, :]
    key_doc = doc_index(key_pos.reshape(-1), doc_ends).reshape(key_pos.shape)
    allowed = (
        (key_pos[:, None, :] <= half_pos[:, :, None])
        & (key_pos[:, None, :] >= 0)
        & (key_doc[:, None, :] == doc_ids.reshape(2, rows)[:, :, None])
    )
    bias = jnp.where(allowed, 0.0, masked_score)
    spare = -width % 128
    even_rows = jnp.pad(block_rows, ((0, 0), (0, spare)))
    odd_rows = jnp.pad(block_rows, ((0, 0), (spare, 0)))

    def attention(place, dtype):
        keys = pl.BlockSpec((row_count, width + spare), lambda i, at: (0, 0))
        return pl.pallas_call(
            functools.partial(
                latent_attention,
                width=width,
                first_key=first_key,
                score_scale=1.0 / math.sqrt(NOPE + ROPE),
            ),
            grid_spec=pltpu.PrefetchScalarGridSpec(
                num_scalar_prefetch=1,
                grid=(steps,),
                in_specs=[
                    pl.BlockSpec((1, rows, HEADS_STEP * width), lambda i, at: (0, at[0], i)),
                    keys,
                    keys,
                    pl.BlockSpec((1, rows, back + rows), lambda i, at: (at[0], 0, 0)),
                    pl.BlockSpec((HEADS_STEP,) + value_up.shape[1:], lambda i, at: (i, 0, 0)),
                    pl.BlockSpec((HEADS_STEP * vhead, model), lambda i, at: (i, 0)),
                ],
                out_specs=pl.BlockSpec((rows, model), lambda i, at: (0, 0)),
                scratch_shapes=[pltpu.VMEM((rows, model), jnp.float32)],
            ),
            out_shape=jax.ShapeDtypeStruct((rows, model), dtype),
            compiler_params=pltpu.CompilerParams(vmem_limit_bytes=48 << 20),
            cost_estimate=pl.CostEstimate(
                flops=12_000_000_000, bytes_accessed=16_000_000, transcendentals=0
            ),
        )(place, in_place(mla_query), even_rows, odd_rows, bias, in_place(value_up), in_place(out_proj))

    def relayed(inbound_state, hop):
        outgoing = offset
        if hop > 0:
            outgoing = offset + jnp.einsum(
                "hcd,hdv->hcv", transition, inbound_state, preferred_element_type=jnp.float32
            )
        return outgoing.astype(jnp.bfloat16)

    head_count = lax.axis_size("head")
    mine = lax.axis_index("head") if head_count == 2 else jnp.int32(1)
    first, outgoing = lax.optimization_barrier(((1 - mine)[None], relayed(None, 0)))
    inbound_state = from_behind(outgoing, "ctx", 1)
    far_part = attention(first, jnp.bfloat16)
    if head_count == 2:
        far_part = lax.ppermute(far_part, "head", [(0, 1), (1, 0)])
    second = mine[None]
    for hop in range(1, hops):
        outgoing = relayed(inbound_state, hop)
        second, outgoing = lax.optimization_barrier((second, outgoing))
        inbound_state = from_behind(outgoing, "ctx", 1)
    if head_count == 2:
        near_part = attention(second, jnp.float32)
        mixed = (near_part + far_part.astype(jnp.float32)).astype(jnp.bfloat16)
    else:
        near_part = attention(second, jnp.bfloat16)
        mixed = lax.psum_scatter(
            jnp.concatenate([far_part, near_part], axis=0),
            "head",
            scatter_dimension=0,
            tiled=True,
        )
    kda_out = pl.pallas_call(
        delta_readout,
        grid=(steps,),
        in_specs=[flat, flat, square],
        out_specs=packed,
        out_shape=jax.ShapeDtypeStruct((1, tokens_dev, heads_dev * state_dim), jnp.bfloat16),
        cost_estimate=pl.CostEstimate(
            flops=100_000_000, bytes_accessed=4_000_000, transcendentals=0
        ),
    )(readout, local_part, inbound_state)
    return (kda_out, mixed[None])


def solution(mesh):
    placed = (
        P(("group", "req"), "ctx", "head"),
        P(("group", "req"), "ctx", "head"),
        P(("group", "req"), "ctx", "head"),
        P(("group", "req"), "ctx", "head"),
        P(("group", "req"), "head", "ctx"),
        P(("group", "req"), "ctx", "head"),
        P(("group", "req"), "ctx", None),
        P("head", None, None),
        P("head", None),
        P(("group", "req"), None),
    )
    return jax.shard_map(
        local,
        mesh=mesh,
        in_specs=placed,
        out_specs=(P(("group", "req"), "ctx", "head"), P(("group", "req"), ("ctx", "head"), None)),
        check_vma=False,
    )
```

```python
import functools
import math

import jax
import jax.numpy as jnp
from jax import lax
from jax.experimental import pallas as pl
from jax.experimental.pallas import tpu as pltpu
from jax.sharding import PartitionSpec as P

ROPE = 64
NOPE = 128
SPAN = 64
HEADS_STEP = 4

masked_score = -1e30
ROWS = (((1,), (0,)), ((), ()))
TRANS = (((1,), (1,)), ((), ()))
OVER = (((0,), (0,)), ((), ()))


def from_behind(value, axis, by):
    peers = lax.axis_size(axis)
    pairs = [(i, i + by) for i in range(peers) if 0 <= i + by < peers]
    return lax.ppermute(value, axis, pairs)


def in_place(value):
    return pltpu.with_memory_space_constraint(value, pltpu.HBM)


def doc_index(position_list, doc_ends):
    return jnp.sum((doc_ends[None, :] <= position_list[:, None]).astype(jnp.int32), axis=1)


def dot_once(left, right, dims):
    return lax.dot_general(
        left.astype(jnp.bfloat16),
        right.astype(jnp.bfloat16),
        dims,
        preferred_element_type=jnp.float32,
    )


def halves(value):
    high = value.astype(jnp.bfloat16)
    return high, (value - high.astype(jnp.float32)).astype(jnp.bfloat16)


def dot_split(left, right, dims):
    left_high, left_low = halves(left)
    right_high, right_low = halves(right)
    return (
        dot_once(left_high, right_low, dims) + dot_once(left_low, right_high, dims)
    ) + dot_once(left_high, right_high, dims)


def delta_terms(
    first_ref,
    lengths_ref,
    query_ref,
    key_ref,
    value_ref,
    decay_ref,
    strength_ref,
    readout_ref,
    local_ref,
    transition_ref,
    offset_ref,
):
    tokens = query_ref.shape[1]
    state_dim = transition_ref.shape[1]
    spans = tokens // SPAN
    heads = range(strength_ref.shape[2])
    row = lax.broadcasted_iota(jnp.int32, (tokens, tokens), 0)
    col = lax.broadcasted_iota(jnp.int32, (tokens, tokens), 1)
    inclusive = jnp.where(row >= col, 1.0, 0.0).astype(jnp.bfloat16)
    first = first_ref[0]
    pos_col = first + lax.broadcasted_iota(jnp.int32, (tokens, 1), 0)
    pos_row = first + lax.broadcasted_iota(jnp.int32, (1, tokens), 1)
    doc_col, doc_row = jnp.zeros_like(pos_col), jnp.zeros_like(pos_row)
    prev_doc, last_doc, end = jnp.int32(0), jnp.int32(0), jnp.int32(0)
    for d in range(lengths_ref.shape[0]):
        end = end + lengths_ref[d]
        doc_col = doc_col + jnp.where(pos_col >= end, 1, 0)
        doc_row = doc_row + jnp.where(pos_row >= end, 1, 0)
        prev_doc = prev_doc + jnp.where(first - 1 >= end, 1, 0)
        last_doc = last_doc + jnp.where(first + tokens - 1 >= end, 1, 0)
    same_doc = doc_col == doc_row
    strict = same_doc & (row > col)
    up_to = same_doc & (row >= col)
    carried = jnp.where(doc_col == prev_doc, 1.0, 0.0)
    tail = jnp.where(doc_col == last_doc, 1.0, 0.0)
    small_row = lax.broadcasted_iota(jnp.int32, (SPAN, SPAN), 0)
    small_col = lax.broadcasted_iota(jnp.int32, (SPAN, SPAN), 1)
    queries, keys, strengths, summed = [], [], [], []
    for h in heads:
        lanes = slice(h * state_dim, (h + 1) * state_dim)
        query = query_ref[0, :, lanes].astype(jnp.float32)
        key = key_ref[0, :, lanes].astype(jnp.float32)
        queries.append(query * lax.rsqrt(jnp.sum(query * query, axis=1, keepdims=True) + 1e-06))
        keys.append(key * lax.rsqrt(jnp.sum(key * key, axis=1, keepdims=True) + 1e-06))
        strengths.append(strength_ref[0, :, h : h + 1])
        summed.append(dot_once(inclusive, decay_ref[0, :, lanes], ROWS))
    attends, lowers = [], []
    for h in heads:
        attend_rows, lower_rows = [], []
        for a in range(spans):
            here = slice(a * SPAN, (a + 1) * SPAN)
            seen = (a + 1) * SPAN
            if a == 0:
                start = jnp.zeros((1, state_dim), jnp.float32)
            else:
                start = summed[h][a * SPAN - 1 : a * SPAN]
            fall = jnp.exp(summed[h][here] - start)
            stacked = jnp.concatenate([keys[h][here] * fall, queries[h][here] * fall], axis=0)
            lifted = keys[h][:seen] * jnp.exp(start - summed[h][:seen])
            both = dot_split(stacked, lifted, TRANS)
            lower_rows.append(
                jnp.where(strict[here, :seen], both[:SPAN] * strengths[h][here], 0.0)
            )
            attend_rows.append(jnp.where(up_to[here, :seen], both[SPAN:], 0.0))
        attends.append(attend_rows)
        lowers.append(lower_rows)
    inverses = [[None] * spans for _ in heads]
    width = 1
    while width < SPAN:
        corner = (small_row // (2 * width) == small_col // (2 * width)) & (
            small_row // width > small_col // width
        )
        cells = [(h, a) for h in heads for a in range(spans)]
        parts = {
            (h, a): jnp.where(corner, lowers[h][a][:, a * SPAN :], 0.0) for h, a in cells
        }
        if width == 1:
            for h, a in cells:
                inverses[h][a] = -parts[h, a]
        else:
            lefts = {
                (h, a): parts[h, a] + dot_once(inverses[h][a], parts[h, a], ROWS)
                for h, a in cells
            }
            for h, a in cells:
                inverses[h][a] = inverses[h][a] - (
                    lefts[h, a] + dot_once(lefts[h, a], inverses[h][a], ROWS)
                )
        width *= 2
    solved = [[] for _ in heads]
    growths = [jnp.exp(summed[h]) for h in heads]
    for a in range(spans):
        here = slice(a * SPAN, (a + 1) * SPAN)
        for h in heads:
            lanes = slice(h * state_dim, (h + 1) * state_dim)
            right = strengths[h][here] * jnp.concatenate(
                [
                    carried[here] * keys[h][here] * growths[h][here],
                    value_ref[0, here, lanes].astype(jnp.float32),
                ],
                axis=1,
            )
            if a > 0:
                before = jnp.concatenate(solved[h], axis=0) if a > 1 else solved[h][0]
                right = right - dot_once(lowers[h][a][:, : a * SPAN], before, ROWS)
            solved[h].append(right + dot_once(inverses[h][a], right, ROWS))
    eye = jnp.where(
        lax.broadcasted_iota(jnp.int32, (state_dim, state_dim), 0)
        == lax.broadcasted_iota(jnp.int32, (state_dim, state_dim), 1),
        1.0,
        0.0,
    )
    for h in heads:
        lanes = slice(h * state_dim, (h + 1) * state_dim)
        whole = jnp.concatenate(solved[h], axis=0)
        for a in range(spans):
            here = slice(a * SPAN, (a + 1) * SPAN)
            seen = (a + 1) * SPAN
            read = dot_once(attends[h][a], whole[:seen], ROWS)
            readout_ref[here, lanes] = (
                carried[here] * queries[h][here] * growths[h][here] - read[:, :state_dim]
            ).astype(readout_ref.dtype)
            local_ref[here, lanes] = read[:, state_dim:]
        last = summed[h][tokens - 1 : tokens]
        key_decay = keys[h] * jnp.exp(last - summed[h]) * tail
        moved = dot_once(key_decay, whole, OVER)
        kept = carried[tokens - 1 : tokens] * growths[h][tokens - 1 : tokens]
        transition_ref[h] = (eye * kept - moved[:, :state_dim]).astype(transition_ref.dtype)
        offset_ref[h] = moved[:, state_dim:]


def delta_readout(readout_ref, local_ref, state_ref, out_ref):
    state_dim = state_ref.shape[1]
    for h in range(state_ref.shape[0]):
        lanes = slice(h * state_dim, (h + 1) * state_dim)
        out_ref[0, :, lanes] = (
            local_ref[:, lanes]
            + jnp.dot(readout_ref[:, lanes], state_ref[h], preferred_element_type=jnp.float32)
        ).astype(out_ref.dtype)


def latent_attention(
    place_ref,
    query_ref,
    even_ref,
    odd_ref,
    bias_ref,
    up_ref,
    proj_ref,
    out_ref,
    total_ref,
    *,
    width,
    first_key,
    score_scale,
):
    rows = query_ref.shape[1]
    key_count = bias_ref.shape[2]
    keys = pl.ds(pl.multiple_of(place_ref[0] * rows + first_key, math.gcd(rows, 16)), key_count)
    lat_dim = up_ref.shape[1]
    pairs = up_ref.shape[0] // 2
    wide = even_ref.shape[1]
    bias = bias_ref[0]
    bias = jnp.concatenate([bias] * pairs, axis=0) if pairs > 1 else bias
    contexts = []
    for key_ref, skip in ((even_ref, 0), (odd_ref, 2 * width - wide)):
        stacked = [
            query_ref[0, :, 2 * p * width + skip : 2 * p * width + skip + wide]
            for p in range(pairs)
        ]
        query = jnp.concatenate(stacked, axis=0) if pairs > 1 else stacked[0]
        scores = lax.dot_general(
            query, key_ref[keys, :], TRANS, preferred_element_type=jnp.float32
        )
        scores = scores * score_scale + bias
        exponent = jnp.exp(scores - jnp.max(scores, axis=1, keepdims=True))
        row_total = jnp.sum(exponent, axis=1, keepdims=True)
        weighted = jnp.dot(
            exponent.astype(jnp.bfloat16),
            even_ref[keys, :lat_dim],
            preferred_element_type=jnp.float32,
        )
        contexts.append((weighted / row_total).astype(jnp.bfloat16))
    head_out = []
    for p in range(pairs):
        for parity in range(2):
            head_out.append(
                jnp.dot(
                    contexts[parity][p * rows : (p + 1) * rows],
                    up_ref[2 * p + parity],
                    preferred_element_type=jnp.float32,
                ).astype(jnp.bfloat16)
            )
    part = jnp.dot(
        jnp.concatenate(head_out, axis=1), proj_ref[...], preferred_element_type=jnp.float32
    )
    step = pl.program_id(0)

    @pl.when(step == 0)
    def _():
        total_ref[...] = part

    @pl.when(step > 0)
    def _():
        total_ref[...] += part

    @pl.when(step == pl.num_programs(0) - 1)
    def _():
        out_ref[...] = total_ref[...].astype(out_ref.dtype)


def local(
    kda_query,
    kda_key,
    kda_value,
    log_decay,
    write_strength,
    mla_query,
    latents,
    value_up,
    out_proj,
    doc_lengths,
):
    tokens_dev = kda_query.shape[1]
    heads_dev = write_strength.shape[1]
    state_dim = kda_query.shape[2] // heads_dev
    ctx_count = lax.axis_size("ctx")
    ctx_place = lax.axis_index("ctx")
    longest = 3 * tokens_dev * ctx_count // 8
    hops = min(ctx_count - 1, -(-(longest - 1) // tokens_dev))
    first_pos = ctx_place * tokens_dev
    positions = first_pos + jnp.arange(tokens_dev, dtype=jnp.int32)
    order = jnp.arange(doc_lengths.shape[1], dtype=jnp.int32)
    doc_ends = jnp.sum(jnp.where(order[None, :] <= order[:, None], doc_lengths, 0), axis=1)
    doc_ids = doc_index(positions, doc_ends)
    window = [from_behind(latents[0], "ctx", by) for by in range(hops, 0, -1)]
    block_rows = jnp.concatenate(window + [latents[0]], axis=0)

    steps = heads_dev // HEADS_STEP
    lanes_step = HEADS_STEP * state_dim
    strength = jnp.transpose(
        write_strength[0].reshape(steps, HEADS_STEP, tokens_dev), (0, 2, 1)
    )
    packed = pl.BlockSpec((1, tokens_dev, lanes_step), lambda i, *_: (0, 0, i))
    flat = pl.BlockSpec((tokens_dev, lanes_step), lambda i, *_: (0, i))
    square = pl.BlockSpec((HEADS_STEP, state_dim, state_dim), lambda i, *_: (i, 0, 0))
    readout, local_part, transition, offset = pl.pallas_call(
        delta_terms,
        grid_spec=pltpu.PrefetchScalarGridSpec(
            num_scalar_prefetch=2,
            grid=(steps,),
            in_specs=[packed] * 4
            + [pl.BlockSpec((1, tokens_dev, HEADS_STEP), lambda i, *_: (i, 0, 0))],
            out_specs=[flat, flat, square, square],
        ),
        out_shape=[
            pltpu.HBM((tokens_dev, heads_dev * state_dim), jnp.bfloat16),
            pltpu.HBM((tokens_dev, heads_dev * state_dim), jnp.float32),
            jax.ShapeDtypeStruct((heads_dev, state_dim, state_dim), jnp.bfloat16),
            jax.ShapeDtypeStruct((heads_dev, state_dim, state_dim), jnp.float32),
        ],
        compiler_params=pltpu.CompilerParams(vmem_limit_bytes=48 << 20),
        cost_estimate=pl.CostEstimate(
            flops=20_000_000_000, bytes_accessed=8_000_000, transcendentals=0
        ),
    )(
        first_pos[None],
        doc_lengths[0],
        in_place(kda_query),
        in_place(kda_key),
        in_place(kda_value),
        in_place(log_decay),
        strength,
    )

    width = latents.shape[2]
    vhead = value_up.shape[2]
    model = out_proj.shape[1]
    row_count = block_rows.shape[0]
    rows = tokens_dev // 2
    back = -(-(longest - 1) // rows) * rows
    first_key = hops * tokens_dev - back
    half_pos = positions.reshape(2, rows)
    key_pos = half_pos[:, :1] - back + jnp.arange(back + rows, dtype=jnp.int32)[None, :]
    key_doc = doc_index(key_pos.reshape(-1), doc_ends).reshape(key_pos.shape)
    allowed = (
        (key_pos[:, None, :] <= half_pos[:, :, None])
        & (key_pos[:, None, :] >= 0)
        & (key_doc[:, None, :] == doc_ids.reshape(2, rows)[:, :, None])
    )
    bias = jnp.where(allowed, 0.0, masked_score)
    spare = -width % 128
    even_rows = jnp.pad(block_rows, ((0, 0), (0, spare)))
    odd_rows = jnp.pad(block_rows, ((0, 0), (spare, 0)))

    def attention(place, dtype):
        keys = pl.BlockSpec((row_count, width + spare), lambda i, at: (0, 0))
        return pl.pallas_call(
            functools.partial(
                latent_attention,
                width=width,
                first_key=first_key,
                score_scale=1.0 / math.sqrt(NOPE + ROPE),
            ),
            grid_spec=pltpu.PrefetchScalarGridSpec(
                num_scalar_prefetch=1,
                grid=(steps,),
                in_specs=[
                    pl.BlockSpec((1, rows, HEADS_STEP * width), lambda i, at: (0, at[0], i)),
                    keys,
                    keys,
                    pl.BlockSpec((1, rows, back + rows), lambda i, at: (at[0], 0, 0)),
                    pl.BlockSpec((HEADS_STEP,) + value_up.shape[1:], lambda i, at: (i, 0, 0)),
                    pl.BlockSpec((HEADS_STEP * vhead, model), lambda i, at: (i, 0)),
                ],
                out_specs=pl.BlockSpec((rows, model), lambda i, at: (0, 0)),
                scratch_shapes=[pltpu.VMEM((rows, model), jnp.float32)],
            ),
            out_shape=jax.ShapeDtypeStruct((rows, model), dtype),
            compiler_params=pltpu.CompilerParams(vmem_limit_bytes=48 << 20),
            cost_estimate=pl.CostEstimate(
                flops=12_000_000_000, bytes_accessed=16_000_000, transcendentals=0
            ),
        )(place, in_place(mla_query), even_rows, odd_rows, bias, in_place(value_up), in_place(out_proj))

    def relayed(inbound_state, hop):
        outgoing = offset
        if hop > 0:
            outgoing = offset + jnp.einsum(
                "hcd,hdv->hcv", transition, inbound_state, preferred_element_type=jnp.float32
            )
        return outgoing.astype(jnp.bfloat16)

    head_count = lax.axis_size("head")
    mine = lax.axis_index("head") if head_count == 2 else jnp.int32(1)
    first, outgoing = lax.optimization_barrier(((1 - mine)[None], relayed(None, 0)))
    inbound_state = from_behind(outgoing, "ctx", 1)
    far_part = attention(first, jnp.bfloat16)
    if head_count == 2:
        far_part = lax.ppermute(far_part, "head", [(0, 1), (1, 0)])
    second = mine[None]
    for hop in range(1, hops):
        outgoing = relayed(inbound_state, hop)
        second, outgoing = lax.optimization_barrier((second, outgoing))
        inbound_state = from_behind(outgoing, "ctx", 1)
    if head_count == 2:
        near_part = attention(second, jnp.float32)
        mixed = (near_part + far_part.astype(jnp.float32)).astype(jnp.bfloat16)
    else:
        near_part = attention(second, jnp.bfloat16)
        mixed = lax.psum_scatter(
            jnp.concatenate([far_part, near_part], axis=0),
            "head",
            scatter_dimension=0,
            tiled=True,
        )
    kda_out = pl.pallas_call(
        delta_readout,
        grid=(steps,),
        in_specs=[flat, flat, square],
        out_specs=packed,
        out_shape=jax.ShapeDtypeStruct((1, tokens_dev, heads_dev * state_dim), jnp.bfloat16),
        cost_estimate=pl.CostEstimate(
            flops=100_000_000, bytes_accessed=4_000_000, transcendentals=0
        ),
    )(readout, local_part, inbound_state)
    return (kda_out, mixed[None])


def solution(mesh):
    placed = (
        P(("group", "req"), "ctx", "head"),
        P(("group", "req"), "ctx", "head"),
        P(("group", "req"), "ctx", "head"),
        P(("group", "req"), "ctx", "head"),
        P(("group", "req"), "head", "ctx"),
        P(("group", "req"), "ctx", "head"),
        P(("group", "req"), "ctx", None),
        P("head", None, None),
        P("head", None),
        P(("group", "req"), None),
    )
    return jax.shard_map(
        local,
        mesh=mesh,
        in_specs=placed,
        out_specs=(P(("group", "req"), "ctx", "head"), P(("group", "req"), ("ctx", "head"), None)),
        check_vma=False,
    )
```

```python
import functools
import math

import jax
import jax.numpy as jnp
from jax import lax
from jax.experimental import pallas as pl
from jax.experimental.pallas import tpu as pltpu
from jax.sharding import PartitionSpec as P

ROPE = 64
NOPE = 128
SPAN = 64
HEADS_STEP = 4

masked_score = -1e30
ROWS = (((1,), (0,)), ((), ()))
TRANS = (((1,), (1,)), ((), ()))
OVER = (((0,), (0,)), ((), ()))


def from_behind(value, axis, by):
    peers = lax.axis_size(axis)
    pairs = [(i, i + by) for i in range(peers) if 0 <= i + by < peers]
    return lax.ppermute(value, axis, pairs)


def in_place(value):
    return pltpu.with_memory_space_constraint(value, pltpu.HBM)


def doc_index(position_list, doc_ends):
    return jnp.sum((doc_ends[None, :] <= position_list[:, None]).astype(jnp.int32), axis=1)


def dot_once(left, right, dims):
    return lax.dot_general(
        left.astype(jnp.bfloat16),
        right.astype(jnp.bfloat16),
        dims,
        preferred_element_type=jnp.float32,
    )


def halves(value):
    high = value.astype(jnp.bfloat16)
    return high, (value - high.astype(jnp.float32)).astype(jnp.bfloat16)


def dot_split(left, right, dims):
    left_high, left_low = halves(left)
    right_high, right_low = halves(right)
    return (
        dot_once(left_high, right_low, dims) + dot_once(left_low, right_high, dims)
    ) + dot_once(left_high, right_high, dims)


def delta_terms(
    first_ref,
    lengths_ref,
    query_ref,
    key_ref,
    value_ref,
    decay_ref,
    strength_ref,
    readout_ref,
    local_ref,
    transition_ref,
    offset_ref,
):
    tokens = query_ref.shape[1]
    state_dim = transition_ref.shape[1]
    spans = tokens // SPAN
    heads = range(strength_ref.shape[2])
    row = lax.broadcasted_iota(jnp.int32, (tokens, tokens), 0)
    col = lax.broadcasted_iota(jnp.int32, (tokens, tokens), 1)
    inclusive = jnp.where(row >= col, 1.0, 0.0).astype(jnp.bfloat16)
    first = first_ref[0]
    pos_col = first + lax.broadcasted_iota(jnp.int32, (tokens, 1), 0)
    pos_row = first + lax.broadcasted_iota(jnp.int32, (1, tokens), 1)
    doc_col, doc_row = jnp.zeros_like(pos_col), jnp.zeros_like(pos_row)
    prev_doc, last_doc, end = jnp.int32(0), jnp.int32(0), jnp.int32(0)
    for d in range(lengths_ref.shape[0]):
        end = end + lengths_ref[d]
        doc_col = doc_col + jnp.where(pos_col >= end, 1, 0)
        doc_row = doc_row + jnp.where(pos_row >= end, 1, 0)
        prev_doc = prev_doc + jnp.where(first - 1 >= end, 1, 0)
        last_doc = last_doc + jnp.where(first + tokens - 1 >= end, 1, 0)
    same_doc = doc_col == doc_row
    strict = same_doc & (row > col)
    up_to = same_doc & (row >= col)
    carried = jnp.where(doc_col == prev_doc, 1.0, 0.0)
    tail = jnp.where(doc_col == last_doc, 1.0, 0.0)
    small_row = lax.broadcasted_iota(jnp.int32, (SPAN, SPAN), 0)
    small_col = lax.broadcasted_iota(jnp.int32, (SPAN, SPAN), 1)
    queries, keys, strengths, summed = [], [], [], []
    for h in heads:
        lanes = slice(h * state_dim, (h + 1) * state_dim)
        query = query_ref[0, :, lanes].astype(jnp.float32)
        key = key_ref[0, :, lanes].astype(jnp.float32)
        queries.append(query * lax.rsqrt(jnp.sum(query * query, axis=1, keepdims=True) + 1e-06))
        keys.append(key * lax.rsqrt(jnp.sum(key * key, axis=1, keepdims=True) + 1e-06))
        strengths.append(strength_ref[0, :, h : h + 1])
        summed.append(dot_once(inclusive, decay_ref[0, :, lanes], ROWS))
    attends, lowers = [], []
    for h in heads:
        attend_rows, lower_rows = [], []
        for a in range(spans):
            here = slice(a * SPAN, (a + 1) * SPAN)
            seen = (a + 1) * SPAN
            if a == 0:
                start = jnp.zeros((1, state_dim), jnp.float32)
            else:
                start = summed[h][a * SPAN - 1 : a * SPAN]
            fall = jnp.exp(summed[h][here] - start)
            stacked = jnp.concatenate([keys[h][here] * fall, queries[h][here] * fall], axis=0)
            lifted = keys[h][:seen] * jnp.exp(start - summed[h][:seen])
            both = dot_split(stacked, lifted, TRANS)
            lower_rows.append(
                jnp.where(strict[here, :seen], both[:SPAN] * strengths[h][here], 0.0)
            )
            attend_rows.append(jnp.where(up_to[here, :seen], both[SPAN:], 0.0))
        attends.append(attend_rows)
        lowers.append(lower_rows)
    inverses = [[None] * spans for _ in heads]
    width = 1
    while width < SPAN:
        corner = (small_row // (2 * width) == small_col // (2 * width)) & (
            small_row // width > small_col // width
        )
        cells = [(h, a) for h in heads for a in range(spans)]
        parts = {
            (h, a): jnp.where(corner, lowers[h][a][:, a * SPAN :], 0.0) for h, a in cells
        }
        if width == 1:
            for h, a in cells:
                inverses[h][a] = -parts[h, a]
        else:
            lefts = {
                (h, a): parts[h, a] + dot_once(inverses[h][a], parts[h, a], ROWS)
                for h, a in cells
            }
            for h, a in cells:
                inverses[h][a] = inverses[h][a] - (
                    lefts[h, a] + dot_once(lefts[h, a], inverses[h][a], ROWS)
                )
        width *= 2
    solved = [[] for _ in heads]
    growths = [jnp.exp(summed[h]) for h in heads]
    for a in range(spans):
        here = slice(a * SPAN, (a + 1) * SPAN)
        for h in heads:
            lanes = slice(h * state_dim, (h + 1) * state_dim)
            right = strengths[h][here] * jnp.concatenate(
                [
                    carried[here] * keys[h][here] * growths[h][here],
                    value_ref[0, here, lanes].astype(jnp.float32),
                ],
                axis=1,
            )
            if a > 0:
                before = jnp.concatenate(solved[h], axis=0) if a > 1 else solved[h][0]
                right = right - dot_once(lowers[h][a][:, : a * SPAN], before, ROWS)
            solved[h].append(right + dot_once(inverses[h][a], right, ROWS))
    eye = jnp.where(
        lax.broadcasted_iota(jnp.int32, (state_dim, state_dim), 0)
        == lax.broadcasted_iota(jnp.int32, (state_dim, state_dim), 1),
        1.0,
        0.0,
    )
    for h in heads:
        lanes = slice(h * state_dim, (h + 1) * state_dim)
        whole = jnp.concatenate(solved[h], axis=0)
        for a in range(spans):
            here = slice(a * SPAN, (a + 1) * SPAN)
            seen = (a + 1) * SPAN
            read = dot_once(attends[h][a], whole[:seen], ROWS)
            readout_ref[here, lanes] = (
                carried[here] * queries[h][here] * growths[h][here] - read[:, :state_dim]
            ).astype(readout_ref.dtype)
            local_ref[here, lanes] = read[:, state_dim:]
        last = summed[h][tokens - 1 : tokens]
        key_decay = keys[h] * jnp.exp(last - summed[h]) * tail
        moved = dot_once(key_decay, whole, OVER)
        kept = carried[tokens - 1 : tokens] * growths[h][tokens - 1 : tokens]
        transition_ref[h] = (eye * kept - moved[:, :state_dim]).astype(transition_ref.dtype)
        offset_ref[h] = moved[:, state_dim:]


def delta_readout(readout_ref, local_ref, state_ref, out_ref):
    state_dim = state_ref.shape[1]
    first_head = pl.program_id(0) * HEADS_STEP
    for h in range(HEADS_STEP):
        lanes = slice(h * state_dim, (h + 1) * state_dim)
        out_ref[0, :, lanes] = (
            local_ref[:, lanes]
            + jnp.dot(
                readout_ref[:, lanes],
                state_ref[first_head + h],
                preferred_element_type=jnp.float32,
            )
        ).astype(out_ref.dtype)


def latent_attention(
    place_ref,
    query_ref,
    even_ref,
    odd_ref,
    bias_ref,
    up_ref,
    proj_ref,
    out_ref,
    total_ref,
    *,
    width,
    first_key,
    score_scale,
):
    rows = query_ref.shape[1]
    key_count = bias_ref.shape[2]
    keys = pl.ds(pl.multiple_of(place_ref[0] * rows + first_key, math.gcd(rows, 16)), key_count)
    lat_dim = up_ref.shape[1]
    pairs = up_ref.shape[0] // 2
    wide = even_ref.shape[1]
    bias = bias_ref[0]
    bias = jnp.concatenate([bias] * pairs, axis=0) if pairs > 1 else bias
    contexts = []
    for key_ref, skip in ((even_ref, 0), (odd_ref, 2 * width - wide)):
        stacked = [
            query_ref[0, :, 2 * p * width + skip : 2 * p * width + skip + wide]
            for p in range(pairs)
        ]
        query = jnp.concatenate(stacked, axis=0) if pairs > 1 else stacked[0]
        scores = lax.dot_general(
            query, key_ref[keys, :], TRANS, preferred_element_type=jnp.float32
        )
        scores = scores * score_scale + bias
        exponent = jnp.exp(scores - jnp.max(scores, axis=1, keepdims=True))
        row_total = jnp.sum(exponent, axis=1, keepdims=True)
        weighted = jnp.dot(
            exponent.astype(jnp.bfloat16),
            even_ref[keys, :lat_dim],
            preferred_element_type=jnp.float32,
        )
        contexts.append((weighted / row_total).astype(jnp.bfloat16))
    head_out = []
    for p in range(pairs):
        for parity in range(2):
            head_out.append(
                jnp.dot(
                    contexts[parity][p * rows : (p + 1) * rows],
                    up_ref[2 * p + parity],
                    preferred_element_type=jnp.float32,
                ).astype(jnp.bfloat16)
            )
    part = jnp.dot(
        jnp.concatenate(head_out, axis=1), proj_ref[...], preferred_element_type=jnp.float32
    )
    step = pl.program_id(0)

    @pl.when(step == 0)
    def _():
        total_ref[...] = part

    @pl.when(step > 0)
    def _():
        total_ref[...] += part

    @pl.when(step == pl.num_programs(0) - 1)
    def _():
        out_ref[...] = total_ref[...].astype(out_ref.dtype)


def local(
    kda_query,
    kda_key,
    kda_value,
    log_decay,
    write_strength,
    mla_query,
    latents,
    value_up,
    out_proj,
    doc_lengths,
):
    tokens_dev = kda_query.shape[1]
    heads_dev = write_strength.shape[1]
    state_dim = kda_query.shape[2] // heads_dev
    ctx_count = lax.axis_size("ctx")
    ctx_place = lax.axis_index("ctx")
    longest = 3 * tokens_dev * ctx_count // 8
    hops = min(ctx_count - 1, -(-(longest - 1) // tokens_dev))
    first_pos = ctx_place * tokens_dev
    positions = first_pos + jnp.arange(tokens_dev, dtype=jnp.int32)
    order = jnp.arange(doc_lengths.shape[1], dtype=jnp.int32)
    doc_ends = jnp.sum(jnp.where(order[None, :] <= order[:, None], doc_lengths, 0), axis=1)
    doc_ids = doc_index(positions, doc_ends)
    window = [from_behind(latents[0], "ctx", by) for by in range(hops, 0, -1)]
    block_rows = jnp.concatenate(window + [latents[0]], axis=0)

    steps = heads_dev // HEADS_STEP
    lanes_step = HEADS_STEP * state_dim
    strength = jnp.transpose(
        write_strength[0].reshape(steps, HEADS_STEP, tokens_dev), (0, 2, 1)
    )
    packed = pl.BlockSpec((1, tokens_dev, lanes_step), lambda i, *_: (0, 0, i))
    flat = pl.BlockSpec((tokens_dev, lanes_step), lambda i, *_: (0, i))
    square = pl.BlockSpec((HEADS_STEP, state_dim, state_dim), lambda i, *_: (i, 0, 0))
    readout, local_part, transition, offset = pl.pallas_call(
        delta_terms,
        grid_spec=pltpu.PrefetchScalarGridSpec(
            num_scalar_prefetch=2,
            grid=(steps,),
            in_specs=[packed] * 4
            + [pl.BlockSpec((1, tokens_dev, HEADS_STEP), lambda i, *_: (i, 0, 0))],
            out_specs=[flat, flat, square, square],
        ),
        out_shape=[
            pltpu.HBM((tokens_dev, heads_dev * state_dim), jnp.bfloat16),
            pltpu.HBM((tokens_dev, heads_dev * state_dim), jnp.float32),
            jax.ShapeDtypeStruct((heads_dev, state_dim, state_dim), jnp.bfloat16),
            jax.ShapeDtypeStruct((heads_dev, state_dim, state_dim), jnp.float32),
        ],
        compiler_params=pltpu.CompilerParams(vmem_limit_bytes=48 << 20),
        cost_estimate=pl.CostEstimate(
            flops=20_000_000_000, bytes_accessed=8_000_000, transcendentals=0
        ),
    )(
        first_pos[None],
        doc_lengths[0],
        in_place(kda_query),
        in_place(kda_key),
        in_place(kda_value),
        in_place(log_decay),
        strength,
    )

    width = latents.shape[2]
    vhead = value_up.shape[2]
    model = out_proj.shape[1]
    row_count = block_rows.shape[0]
    rows = tokens_dev // 2
    back = -(-(longest - 1) // rows) * rows
    first_key = hops * tokens_dev - back
    half_pos = positions.reshape(2, rows)
    key_pos = half_pos[:, :1] - back + jnp.arange(back + rows, dtype=jnp.int32)[None, :]
    key_doc = doc_index(key_pos.reshape(-1), doc_ends).reshape(key_pos.shape)
    allowed = (
        (key_pos[:, None, :] <= half_pos[:, :, None])
        & (key_pos[:, None, :] >= 0)
        & (key_doc[:, None, :] == doc_ids.reshape(2, rows)[:, :, None])
    )
    bias = jnp.where(allowed, 0.0, masked_score)
    spare = -width % 128
    even_rows = jnp.pad(block_rows, ((0, 0), (0, spare)))
    odd_rows = jnp.pad(block_rows, ((0, 0), (spare, 0)))

    def attention(place, dtype):
        keys = pl.BlockSpec((row_count, width + spare), lambda i, at: (0, 0))
        return pl.pallas_call(
            functools.partial(
                latent_attention,
                width=width,
                first_key=first_key,
                score_scale=1.0 / math.sqrt(NOPE + ROPE),
            ),
            grid_spec=pltpu.PrefetchScalarGridSpec(
                num_scalar_prefetch=1,
                grid=(steps,),
                in_specs=[
                    pl.BlockSpec((1, rows, HEADS_STEP * width), lambda i, at: (0, at[0], i)),
                    keys,
                    keys,
                    pl.BlockSpec((1, rows, back + rows), lambda i, at: (at[0], 0, 0)),
                    pl.BlockSpec((HEADS_STEP,) + value_up.shape[1:], lambda i, at: (i, 0, 0)),
                    pl.BlockSpec((HEADS_STEP * vhead, model), lambda i, at: (i, 0)),
                ],
                out_specs=pl.BlockSpec((rows, model), lambda i, at: (0, 0)),
                scratch_shapes=[pltpu.VMEM((rows, model), jnp.float32)],
            ),
            out_shape=jax.ShapeDtypeStruct((rows, model), dtype),
            compiler_params=pltpu.CompilerParams(vmem_limit_bytes=48 << 20),
            cost_estimate=pl.CostEstimate(
                flops=12_000_000_000, bytes_accessed=16_000_000, transcendentals=0
            ),
        )(place, in_place(mla_query), even_rows, odd_rows, bias, in_place(value_up), in_place(out_proj))

    def relayed(inbound_state, hop):
        outgoing = offset
        if hop > 0:
            outgoing = offset + jnp.einsum(
                "hcd,hdv->hcv", transition, inbound_state, preferred_element_type=jnp.float32
            )
        return outgoing.astype(jnp.bfloat16)

    head_count = lax.axis_size("head")
    mine = lax.axis_index("head") if head_count == 2 else jnp.int32(1)
    first, outgoing = lax.optimization_barrier(((1 - mine)[None], relayed(None, 0)))
    inbound_state = from_behind(outgoing, "ctx", 1)
    far_part = attention(first, jnp.bfloat16)
    if head_count == 2:
        far_part = lax.ppermute(far_part, "head", [(0, 1), (1, 0)])
    second = mine[None]
    for hop in range(1, hops):
        outgoing = relayed(inbound_state, hop)
        second, outgoing = lax.optimization_barrier((second, outgoing))
        inbound_state = from_behind(outgoing, "ctx", 1)
    if head_count == 2:
        near_part = attention(second, jnp.float32)
        mixed = (near_part + far_part.astype(jnp.float32)).astype(jnp.bfloat16)
    else:
        near_part = attention(second, jnp.bfloat16)
        mixed = lax.psum_scatter(
            jnp.concatenate([far_part, near_part], axis=0),
            "head",
            scatter_dimension=0,
            tiled=True,
        )
    kda_out = pl.pallas_call(
        delta_readout,
        grid=(steps,),
        in_specs=[flat, flat, pl.BlockSpec(memory_space=pltpu.VMEM)],
        out_specs=packed,
        out_shape=jax.ShapeDtypeStruct((1, tokens_dev, heads_dev * state_dim), jnp.bfloat16),
        cost_estimate=pl.CostEstimate(
            flops=100_000_000, bytes_accessed=4_000_000, transcendentals=0
        ),
    )(readout, local_part, pltpu.with_memory_space_constraint(inbound_state, pltpu.VMEM))
    return (kda_out, mixed[None])


def solution(mesh):
    placed = (
        P(("group", "req"), "ctx", "head"),
        P(("group", "req"), "ctx", "head"),
        P(("group", "req"), "ctx", "head"),
        P(("group", "req"), "ctx", "head"),
        P(("group", "req"), "head", "ctx"),
        P(("group", "req"), "ctx", "head"),
        P(("group", "req"), "ctx", None),
        P("head", None, None),
        P("head", None),
        P(("group", "req"), None),
    )
    return jax.shard_map(
        local,
        mesh=mesh,
        in_specs=placed,
        out_specs=(P(("group", "req"), "ctx", "head"), P(("group", "req"), ("ctx", "head"), None)),
        check_vma=False,
    )
```
